32 devices in a mesh: sub: 8 (over z, x), blk: 4 (over y, core).
Axes of the slice: x: 2, y: 2, z: 4, core: 2. Of those that a mesh axis runs over, the one named last changes fastest.
Arguments:
- a_tiles: bfloat16 [768, 12, 128, 128], P(('sub', 'blk'))
- modes: bfloat16 [768, 16, 128], P(('sub', 'blk')), may hold values from -6 to 6
- col_tiles: int32 [768, 12], P(('sub', 'blk')), may hold values from 0 to 221, as said below
- fetch_list: int32 [32, 126], P(('sub', 'blk')), may hold values from 0 to 767, as said below
Outputs:
- prolong: bfloat16 [768, 12, 16, 128], P(('sub', 'blk'))
- coarse_diag: float32 [768, 256], P('sub')
The draws below stay inside these ranges and needn't reach their ends.
Inputs may be any that keep to these rules, and one draw needn't show every extreme that they name: `col_tiles`: slot 0 of row tile t names t itself (its index within its group); the other slots name other tiles of the same group (values below 96) or 96 + h for entry h of the device's fetch list; every entry of a device's fetch list is named by some slot of that device's rows. `fetch_list`: A device's list is 7 blocks of 18 entries; each block names distinct tiles of one group other than the device's own, different blocks name different groups; tile i of group g has number g * 96 + i.
All inputs are finite; a program needn't handle non-finite values.
Results may differ from the reference program's by a relative error of at most 0.008.
Values may be sent and summed in bfloat16 or wider, within the bound.
No kernel may reach another device: no remote copies, remote signals or barrier semaphores. Data moves between devices by JAX's collectives and lax.ppermute only.
A program may use at most 64 MiB of HBM per device.

```python
import jax
import jax.numpy as jnp
from jax import lax

TILE_DEV = 24
SLOTS = 12
TILE_ROWS = 128
MODES = 16
PEERS = 7
PER_PEER = 18
GHOSTS = 126
GROUP = 96
TILES = 768
N_SUB = 8
N_BLK = 4


def draw_a_tiles(key, part):
    first_key, second_key = jax.random.split(key, 2)
    shape = (TILES, SLOTS, TILE_ROWS, TILE_ROWS)
    offdiag = jax.random.normal(first_key, shape, jnp.float32) * TILE_ROWS ** (-0.5)
    diagonal = jax.random.uniform(second_key, shape, jnp.float32, 1.0, 3.0)
    slot_index = lax.broadcasted_iota(jnp.int32, shape, 1)
    row_index = lax.broadcasted_iota(jnp.int32, shape, 2)
    col_index = lax.broadcasted_iota(jnp.int32, shape, 3)
    values = jnp.where((slot_index == 0) & (row_index == col_index), diagonal, offdiag)
    return values.astype(jnp.bfloat16)


def draw_col_tiles(key, part):

    def per_device(device):
        first_key, second_key = jax.random.split(jax.random.fold_in(key, device))
        count = TILE_DEV * (SLOTS - 1)
        order = jax.random.permutation(first_key, count)
        random_rows = jax.random.randint(second_key, (count,), 0, GROUP - 1)
        itself = device % N_BLK * TILE_DEV + jnp.repeat(jnp.arange(TILE_DEV, dtype=jnp.int32), SLOTS - 1)
        others = random_rows + (random_rows >= itself).astype(jnp.int32)
        filled = jnp.where(order < GHOSTS, GROUP + order, others).reshape(TILE_DEV, SLOTS - 1)
        leading = device % N_BLK * TILE_DEV + jnp.arange(TILE_DEV, dtype=jnp.int32)
        return jnp.concatenate([leading[:, None], filled], axis=1)
    return jax.vmap(per_device)(jnp.arange(N_SUB * N_BLK, dtype=jnp.int32)).reshape(TILES, SLOTS).astype(jnp.int32)


def draw_fetch_list(key, part):

    def per_device(device):
        group_index = device // N_BLK
        first_key, second_key = jax.random.split(jax.random.fold_in(key, device))
        chosen = jax.random.permutation(first_key, N_SUB - 1)[:PEERS]
        groups = chosen + (chosen >= group_index).astype(jnp.int32)
        group_keys = jax.random.split(second_key, PEERS)

        def members(member_key):
            return jax.random.permutation(member_key, GROUP)[:PER_PEER]
        within = jax.vmap(members)(group_keys)
        return (groups[:, None] * GROUP + within).reshape(GHOSTS)
    return jax.vmap(per_device)(jnp.arange(N_SUB * N_BLK, dtype=jnp.int32)).astype(jnp.int32)


def levels(stream_key, extent, cuts, smallest, high):
    loudness, own = 1.0, jax.random.fold_in(stream_key, 6)
    for dim, blocks in cuts:
        heights = jnp.exp(jax.random.uniform(jax.random.fold_in(own, dim), (blocks,), jnp.float32, smallest / len(cuts), high / len(cuts)))
        loudness = loudness * jnp.repeat(heights, extent[dim] // blocks).reshape([-1 if axis == dim else 1 for axis in range(len(extent))])
    return loudness


def centred(own_key, extent, width, bound, cuts=(), kind=jnp.bfloat16):
    level = levels(own_key, extent, cuts, -0.22, 0.18) if cuts else 1.0
    drawn = jax.random.normal(own_key, extent, jnp.float32) * width * level
    return jnp.minimum(jnp.maximum(drawn, -bound), bound).astype(kind)


def setup_inputs(seed: int = 0) -> dict:
    key_list = jax.random.split(jax.random.key(seed), 5)
    return {
        "a_tiles": draw_a_tiles(jax.random.fold_in(key_list[4], 71), 0),
        "modes": centred(key_list[1], (TILES, MODES, TILE_ROWS), 1.0, 6.0, ((0, 32),)),
        "col_tiles": draw_col_tiles(jax.random.fold_in(key_list[4], 71), 0),
        "fetch_list": draw_fetch_list(jax.random.fold_in(key_list[4], 71), 0),
    }


damping = 2.0 / 3.0


def reference(a_tiles, modes, col_tiles, fetch_list):
    def per_device(coarse_sum, device):
        tiles_here = lax.dynamic_slice_in_dim(a_tiles, device * TILE_DEV, TILE_DEV, 0)
        slots_here = lax.dynamic_slice_in_dim(col_tiles, device * TILE_DEV, TILE_DEV, 0)
        modes_here = lax.dynamic_slice_in_dim(modes, device * TILE_DEV, TILE_DEV, 0)
        fetched = lax.dynamic_index_in_dim(fetch_list, device, 0, keepdims=False)
        group_index = device // N_BLK
        remote = fetched[jnp.clip(slots_here - GROUP, 0, GHOSTS - 1)]
        columns = jnp.where(slots_here < GROUP, group_index * GROUP + slots_here, remote).astype(jnp.int32)
        picked = modes[columns]
        product = jnp.einsum("tkrc,tkmc->tkmr", tiles_here.astype(jnp.float32), picked.astype(jnp.float32),
                             precision=lax.Precision.HIGHEST)
        inverse = 1.0 / jnp.diagonal(tiles_here[:, 0], axis1=1, axis2=2).astype(jnp.float32)
        leading = (jnp.arange(SLOTS) == 0).astype(jnp.float32)
        prolong = (leading[None, :, None, None] * modes_here.astype(jnp.float32)[:, None]
                   - damping * inverse[:, None, None, :] * product).astype(jnp.bfloat16)
        partial_value = jnp.einsum("tkmr,tknr->tkmn", prolong.astype(jnp.float32), product,
                             precision=lax.Precision.HIGHEST) / TILE_ROWS
        coarse_sum = coarse_sum.at[columns.reshape(-1)].add(partial_value.reshape(-1, MODES * MODES))
        return coarse_sum, prolong

    start = jnp.zeros((TILES, MODES * MODES), jnp.float32)
    coarse_diag, prolongs = lax.scan(per_device, start, jnp.arange(N_SUB * N_BLK, dtype=jnp.int32))
    return prolongs.reshape(TILES, SLOTS, MODES, TILE_ROWS), coarse_diag
```

```python
import functools

import jax
import jax.numpy as jnp
from jax import lax
from jax.experimental import pallas as pl
from jax.experimental.pallas import tpu as pltpu
from jax.sharding import PartitionSpec as P

NEIGHBOURS = 26
LANES = 128
BATCH = 8

damping = 2.0 / 3.0

VMEM = pl.BlockSpec(memory_space=pltpu.VMEM)
SMEM = pl.BlockSpec(memory_space=pltpu.SMEM)
PARAMS = pltpu.CompilerParams(vmem_limit_bytes=8 << 20)
NT = (((1,), (1,)), ((), ()))


def xor_permute(x, axis, bit):
    count = lax.axis_size(axis)
    return lax.ppermute(x, axis, [(i, i ^ bit) for i in range(count)])


def flatten_rows(load, rows, modes):
    per_vector = LANES // modes
    lane_block = lax.broadcasted_iota(jnp.int32, (rows, LANES), 1) // modes
    halves = []
    for half in range(modes // per_vector):
        total = jnp.zeros((rows, LANES), jnp.float32)
        for place in range(per_vector):
            value = load(half * per_vector + place)
            if place:
                value = pltpu.roll(value, place * modes, 1)
            total = jnp.where(lane_block == place, value, total)
        halves.append(total)
    return halves


def one_hot_sum(one_hot, value):
    high = value.astype(jnp.bfloat16)
    low = (value - high.astype(jnp.float32)).astype(jnp.bfloat16)
    return jnp.dot(one_hot, high, preferred_element_type=jnp.float32) + jnp.dot(
        one_hot, low, preferred_element_type=jnp.float32
    )


def pick_kernel(count, place_ref, table_ref, far_ref, *out_refs):
    for peer, out_ref in enumerate(out_refs):

        @pl.loop(0, count, unroll=2)
        def _(i):
            out_ref[i] = table_ref[place_ref[peer, i]]
            out_ref[count + i] = far_ref[place_ref[peer, count + i]]


def own_kernel(
    slots, own_place, source, cols_ref, table_ref, a_hbm,
    prolong_ref, weight_ref, sums_ref, lists_ref, counts_ref, a_ref, blocks_ref, arrived,
):
    tile_dev = weight_ref.shape[0]
    mode_count, tile_rows = table_ref.shape[1:]
    pair = 2
    per_step = pair * slots
    diagonal = lax.broadcasted_iota(jnp.int32, (tile_rows, tile_rows), 0) == lax.broadcasted_iota(
        jnp.int32, (tile_rows, tile_rows), 1
    )

    def fetch(step):
        part = pl.ds(step * per_step, per_step)
        return pltpu.make_async_copy(a_hbm.at[part], a_ref.at[part], arrived.at[step])

    @pl.loop(0, tile_dev // pair)
    def _(step):
        fetch(step).start()

    @pl.loop(0, tile_dev // pair)
    def _(step):
        fetch(step).wait()
        stages = []
        for i in range(pair):
            tile = step * pair + i
            first = a_ref[tile * slots].astype(jnp.float32)
            entries = jnp.sum(jnp.where(diagonal, first, 0.0), axis=0, keepdims=True)
            weight = damping * (1.0 / entries)
            weight_ref[pl.ds(tile, 1), :] = weight
            for k in range(slots):
                slot = tile * slots + k
                place = own_place[slot]
                picked = table_ref[jnp.maximum(place, 0)]
                picked = jnp.where(place >= 0, picked, jnp.zeros_like(picked))
                product = lax.dot_general(picked, a_ref[slot], NT, preferred_element_type=jnp.float32)
                smooth = -(weight * product)
                if k == 0:
                    smooth = picked.astype(jnp.float32) + smooth
                smooth = smooth.astype(jnp.bfloat16)
                prolong_ref[slot] = smooth
                stages.append((smooth, product.astype(jnp.bfloat16)))
        for b in range(per_step // BATCH):
            part = stages[b * BATCH : (b + 1) * BATCH]
            block = lax.dot_general(
                jnp.concatenate([s for s, _ in part], axis=0),
                jnp.concatenate([q for _, q in part], axis=0),
                NT,
                preferred_element_type=jnp.float32,
            )
            row = (step * (per_step // BATCH) + b) * BATCH * mode_count
            row = pl.multiple_of(row, BATCH * mode_count)
            for j in range(BATCH):
                value = block[j * mode_count : (j + 1) * mode_count]
                if j:
                    value = pltpu.roll(value, LANES - j * mode_count, 1)
                blocks_ref[pl.ds(row + j * mode_count, mode_count), :] = value

    source_count = counts_ref.shape[0]
    for s in range(source_count):
        counts_ref[s] = 0

    @pl.loop(0, tile_dev * slots)
    def _(slot):
        s = source[slot]

        @pl.when(s >= 0)
        def _():
            at = counts_ref[s]
            lists_ref[s, at] = slot
            counts_ref[s] = at + 1

    total = tile_dev * slots
    halves = flatten_rows(
        lambda m: blocks_ref[pl.ds(m, total, stride=mode_count), :], total, mode_count
    )
    group_size = sums_ref.shape[0]
    one_hot = (
        lax.broadcasted_iota(jnp.int32, (group_size, total), 0) == cols_ref[...]
    ).astype(jnp.bfloat16)
    for half, value in enumerate(halves):
        result = one_hot_sum(one_hot, value) * (1.0 / tile_rows)
        sums_ref[:, half * LANES : (half + 1) * LANES] = result.astype(jnp.bfloat16)


def ghost_kernel(
    slots, pitch, entry, lists_ref, counts_ref, target_ref, index_ref, a_ref, weight_ref, old_ref,
    *refs,
):
    sources = refs[:-3]
    prolong_ref, out_ref, blocks_ref = refs[-3:]
    mode_count, tile_rows = sources[0].shape[1:]
    total = a_ref.shape[0]
    blocks_ref[...] = jnp.zeros_like(blocks_ref)

    for s, table_ref in enumerate(sources):
        count = counts_ref[s]

        @pl.loop(0, (count + BATCH - 1) // BATCH)
        def _(step):
            stages = []
            for i in range(BATCH):
                slot = lists_ref[s, jnp.minimum(step * BATCH + i, count - 1)]
                picked = table_ref[entry[slot]]
                product = lax.dot_general(picked, a_ref[slot], NT, preferred_element_type=jnp.float32)
                weight = weight_ref[pl.ds(slot // slots, 1), :]
                smooth = (-(weight * product)).astype(jnp.bfloat16)
                prolong_ref[slot] = smooth
                stages.append((slot, smooth, product.astype(jnp.bfloat16)))
            for slot, smooth, product in stages:
                block = lax.dot_general(smooth, product, NT, preferred_element_type=jnp.float32)
                row = pl.multiple_of(slot * mode_count, mode_count)
                blocks_ref[pl.ds(row, mode_count), 0:mode_count] = block

    halves = flatten_rows(
        lambda m: blocks_ref[pl.ds(m, total, stride=mode_count), :], total, mode_count
    )
    groups, _, rows, _ = out_ref.shape
    one_hot = (
        lax.broadcasted_iota(jnp.int32, (groups * rows, total), 0) == target_ref[...]
    ).astype(jnp.bfloat16)
    row_place = lax.broadcasted_iota(jnp.int32, (groups, rows, LANES), 1)
    for half, value in enumerate(halves):
        result = one_hot_sum(one_hot, value) * (1.0 / tile_rows)
        result = result.reshape(groups, rows, LANES)
        result = jnp.where(row_place == pitch, index_ref[:, :, half * LANES : (half + 1) * LANES], result)
        result = result.astype(jnp.bfloat16)
        for copy in range(out_ref.shape[1]):
            out_ref[:, copy, :, half * LANES : (half + 1) * LANES] = result


def target_kernel(pitch, incoming_ref, out_ref):
    senders, rows, width = incoming_ref.shape
    group_size = out_ref.shape[0]
    tile = lax.broadcasted_iota(jnp.int32, (group_size, rows), 0)
    total = jnp.zeros((group_size, width), jnp.float32)
    for sender in range(senders):
        value = incoming_ref[sender]
        wanted = value[pitch : pitch + 1, :rows].astype(jnp.float32).astype(jnp.int32)
        one_hot = (tile == wanted).astype(jnp.bfloat16)
        total = total + jnp.dot(one_hot, value, preferred_element_type=jnp.float32)
    out_ref[...] = total.astype(jnp.bfloat16)


def shards(a_tiles, modes, col_tiles, fetch_list):
    blk_count = lax.axis_size("blk")
    sub_count = lax.axis_size("sub")
    tile_dev, slot_count, tile_rows = a_tiles.shape[:3]
    mode_count = modes.shape[1]
    width = mode_count * mode_count
    group_size = tile_dev * blk_count
    ghost_count = fetch_list.shape[1]
    peer_count = min(NEIGHBOURS, sub_count - 1)
    per_peer = ghost_count // peer_count
    slot_total = tile_dev * slot_count
    half = sub_count // 2
    blk_half = blk_count // 2
    me = lax.axis_index("sub")
    lane = lax.axis_index("blk")

    far = xor_permute(modes, "sub", half)
    tables = []
    bits = []
    bit = blk_half
    own_part, far_part = modes[None], far[None]
    while bit:
        own_part = jnp.concatenate([own_part, xor_permute(own_part, "blk", bit)], axis=0)
        far_part = jnp.concatenate([far_part, xor_permute(far_part, "blk", bit)], axis=0)
        bits.append(bit)
        bit //= 2
    own_table = own_part.reshape(group_size, mode_count, tile_rows)
    far_table = far_part.reshape(group_size, mode_count, tile_rows)

    def place_of(within):
        relative = (within // tile_dev) ^ lane
        order = jnp.zeros_like(relative)
        for i, b in enumerate(bits):
            order = order + jnp.where((relative & b) != 0, 1 << i, 0)
        return order * tile_dev + within % tile_dev

    fetched = fetch_list[0]
    places = []
    for peer in range(1, half):
        theirs = xor_permute(fetch_list, "sub", peer)[0].reshape(peer_count, per_peer)
        owner = theirs[:, :1] // group_size
        wanted = theirs % group_size
        near = jnp.sum(jnp.where(owner == me, wanted, 0), axis=0)
        away = jnp.sum(jnp.where(owner == (me ^ half), wanted, 0), axis=0)
        places.append(place_of(jnp.concatenate([near, away])))
    places = jnp.stack(places)

    picks = pl.pallas_call(
        functools.partial(pick_kernel, per_peer),
        out_shape=[jax.ShapeDtypeStruct((2 * per_peer, mode_count, tile_rows), modes.dtype)] * (half - 1),
        in_specs=[SMEM, VMEM, VMEM],
        out_specs=[VMEM] * (half - 1),
        name="pick",
        compiler_params=PARAMS,
    )(places, own_table, far_table)
    received = [xor_permute(picks[peer - 1], "sub", peer) for peer in range(1, half)]

    cols = col_tiles.reshape(slot_total)
    ghost = cols - group_size
    ghost_iota = jnp.arange(ghost_count, dtype=jnp.int32)
    match = ghost[:, None] == ghost_iota[None, :]
    owner_of = fetched // group_size
    apart = owner_of ^ me
    low = apart & (half - 1)
    within = fetched % group_size
    member = ghost_iota % per_peer
    entry_of = jnp.where(low == 0, place_of(within), jnp.where(apart >= half, per_peer, 0) + member)
    rows = -(-(per_peer + 1) // 8) * 8
    row_of = owner_of * rows + member
    packed = (low * group_size * 2 + entry_of) * (sub_count * rows) + row_of
    packed = jnp.sum(jnp.where(match, packed[None, :], 0), axis=1)
    is_ghost = ghost >= 0
    target = jnp.where(is_ghost, packed % (sub_count * rows), -1)
    packed = packed // (sub_count * rows)
    source = jnp.where(is_ghost, packed // (2 * group_size), -1)
    entry = packed % (2 * group_size)
    own_place = jnp.where(is_ghost, -1, place_of(cols))
    index_rows = jnp.sum(
        jnp.where(
            owner_of.reshape(peer_count, per_peer)[:, :1] == jnp.arange(sub_count, dtype=jnp.int32)[None, :],
            1, 0,
        )[:, :, None]
        * (within.reshape(peer_count, per_peer) + 1)[:, None, :],
        axis=0,
    ) - 1
    index_rows = jnp.pad(index_rows, ((0, 0), (0, width - per_peer)), constant_values=-1)
    index_rows = index_rows.astype(jnp.float32).reshape(sub_count, 1, width)

    tiles = a_tiles.reshape(slot_total, tile_rows, tile_rows)
    tiles = pltpu.with_memory_space_constraint(tiles, pltpu.HBM)
    prolong, weight, own_sums, lists, counts, tiles = pl.pallas_call(
        functools.partial(own_kernel, slot_count),
        out_shape=[
            pltpu.VMEM((slot_total, mode_count, tile_rows), jnp.bfloat16),
            jax.ShapeDtypeStruct((tile_dev, tile_rows), jnp.float32),
            jax.ShapeDtypeStruct((group_size, width), jnp.bfloat16),
            jax.ShapeDtypeStruct((half, slot_total), jnp.int32),
            jax.ShapeDtypeStruct((half,), jnp.int32),
            pltpu.VMEM((slot_total, tile_rows, tile_rows), jnp.bfloat16),
        ],
        in_specs=[SMEM, SMEM, VMEM, VMEM, pl.BlockSpec(memory_space=pltpu.HBM)],
        out_specs=[VMEM, VMEM, VMEM, SMEM, SMEM, VMEM],
        scratch_shapes=[
            pltpu.VMEM((slot_total * mode_count, LANES), jnp.float32),
            pltpu.SemaphoreType.DMA((tile_dev // 2,)),
        ],
        name="own",
        compiler_params=PARAMS,
    )(own_place, source, cols[None, :], own_table, tiles)

    prolong = pltpu.with_memory_space_constraint(prolong, pltpu.VMEM)
    tiles = pltpu.with_memory_space_constraint(tiles, pltpu.VMEM)
    own_total = own_sums
    bit = blk_half
    while bit:
        other = xor_permute(own_total, "blk", bit)
        own_total = own_total.astype(jnp.float32) + other.astype(jnp.float32)
        bit //= 2
        if bit:
            own_total = own_total.astype(jnp.bfloat16)

    prolong, outgoing = pl.pallas_call(
        functools.partial(ghost_kernel, slot_count, per_peer),
        out_shape=[
            pltpu.VMEM((slot_total, mode_count, tile_rows), jnp.bfloat16),
            jax.ShapeDtypeStruct((sub_count, blk_half, rows, width), jnp.bfloat16),
        ],
        in_specs=[SMEM, SMEM, SMEM, VMEM, VMEM, VMEM, VMEM, VMEM] + [VMEM] * half,
        out_specs=[VMEM, VMEM],
        input_output_aliases={7: 0},
        scratch_shapes=[pltpu.VMEM((slot_total * mode_count, LANES), jnp.float32)],
        name="ghost",
        compiler_params=PARAMS,
    )(entry, lists, counts, target[None, :], index_rows, tiles, weight, prolong, far_table, *received)

    groups = [
        [s * blk_count + high * 2 + core for s in range(sub_count) for high in range(blk_half)]
        for core in range(2)
    ]
    incoming = lax.all_to_all(
        outgoing.reshape(sub_count * blk_half, rows, width),
        ("sub", "blk"), split_axis=0, concat_axis=0, axis_index_groups=groups, tiled=True,
    )
    arrived = pl.pallas_call(
        functools.partial(target_kernel, per_peer),
        out_shape=jax.ShapeDtypeStruct((group_size, width), jnp.bfloat16),
        in_specs=[VMEM],
        out_specs=VMEM,
        name="target",
        compiler_params=PARAMS,
    )(incoming)
    other = xor_permute(arrived, "blk", 1)
    coarse_diag = own_total + (arrived.astype(jnp.float32) + other.astype(jnp.float32))
    return prolong.reshape(tile_dev, slot_count, mode_count, tile_rows), coarse_diag


def solution(mesh):
    in_specs = (
        P(("sub", "blk"), None, None, None),
        P(("sub", "blk"), None, None),
        P(("sub", "blk"), None),
        P(("sub", "blk"), None),
    )
    out_specs = (P(("sub", "blk"), None, None, None), P("sub", None))
    return jax.shard_map(shards, mesh=mesh, in_specs=in_specs, out_specs=out_specs, check_vma=False)
```

```python
import functools

import jax
import jax.numpy as jnp
from jax import lax
from jax.experimental import pallas as pl
from jax.experimental.pallas import tpu as pltpu
from jax.sharding import PartitionSpec as P

NEIGHBOURS = 26
LANES = 128
BATCH = 8

damping = 2.0 / 3.0

VMEM = pl.BlockSpec(memory_space=pltpu.VMEM)
SMEM = pl.BlockSpec(memory_space=pltpu.SMEM)
PARAMS = pltpu.CompilerParams(vmem_limit_bytes=8 << 20)
NT = (((1,), (1,)), ((), ()))


def xor_permute(x, axis, bit):
    count = lax.axis_size(axis)
    return lax.ppermute(x, axis, [(i, i ^ bit) for i in range(count)])


def divided(value, by):
    return jnp.floor((value.astype(jnp.float32) + 0.5) * (1.0 / by)).astype(jnp.int32)


def table_place(within, lane, tile_dev, bits):
    relative = divided(within, tile_dev)
    rest = within - relative * tile_dev
    relative = relative ^ lane
    order = jnp.zeros_like(relative)
    for i, bit in enumerate(bits):
        order = order + jnp.where((relative & bit) != 0, 1 << i, 0)
    return order * tile_dev + rest


def pick_kernel(count, half, here, owner_ref, place_ref, table_ref, *out_refs):
    for peer, out_ref in enumerate(out_refs):
        near = away = 0
        for p in range(owner_ref.shape[1]):
            owner = owner_ref[peer, p]
            near = jnp.where(owner == here[0], p * count, near)
            away = jnp.where(owner == here[0] ^ half, p * count, away)

        @pl.loop(0, count, unroll=2)
        def _(i):
            out_ref[i] = table_ref[place_ref[peer, near + i]]
            out_ref[count + i] = table_ref[place_ref[peer, away + i]]


def prep_kernel(
    slots, tile_dev, per_peer, rows, half, bits, here,
    cols_ref, fetch_ref, place_ref, row_ref, lists_ref, counts_ref, target_ref, index_ref,
):
    me, lane = here[0], here[1]
    total, ghosts = cols_ref.shape[1], fetch_ref.shape[1]
    group_size = tile_dev * (2 ** len(bits))
    fetched = fetch_ref[...]
    owner = divided(fetched, group_size)
    within = fetched - owner * group_size
    apart = owner ^ me
    low = apart & (half - 1)
    ghost_lane = lax.broadcasted_iota(jnp.int32, (1, ghosts), 1)
    member = ghost_lane - divided(ghost_lane, per_peer) * per_peer
    entry = jnp.where(
        low == 0,
        table_place(within, lane, tile_dev, bits),
        jnp.where(apart >= half, per_peer, 0) + member,
    )
    known = jnp.concatenate([low, entry, owner, member], axis=0).astype(jnp.float32)
    known = known.astype(jnp.bfloat16)
    cols = cols_ref[...]
    match = lax.broadcasted_iota(jnp.int32, (ghosts, total), 0) == cols - group_size
    match = jnp.where(match, 1.0, 0.0).astype(jnp.bfloat16)
    found = jnp.dot(known, match, preferred_element_type=jnp.float32)
    low, entry, owner, member = (found[i : i + 1] for i in range(4))
    is_ghost = cols >= group_size
    source = jnp.where(is_ghost, low.astype(jnp.int32), -1)
    entry_int = entry.astype(jnp.int32)
    place_ref[...] = jnp.where(
        source < 0,
        table_place(cols, lane, tile_dev, bits),
        jnp.where(source == 0, group_size + entry_int, 2 * group_size),
    )
    row_ref[...] = jnp.where(
        source < 0, cols, jnp.where(source == 0, group_size + member.astype(jnp.int32), -1)
    )

    height = -(-half // 8) * 8
    by_source = lax.broadcasted_iota(jnp.int32, (height, total), 0) == source
    by_source = jnp.where(by_source, 1.0, 0.0)
    before = lax.broadcasted_iota(jnp.int32, (total, total), 0) < lax.broadcasted_iota(
        jnp.int32, (total, total), 1
    )
    before = jnp.where(before, 1.0, 0.0).astype(jnp.bfloat16)
    rank = jnp.dot(by_source.astype(jnp.bfloat16), before, preferred_element_type=jnp.float32)
    rank = jnp.where(by_source > 0.5, rank, -1.0).astype(jnp.int32)
    counts = jnp.sum(by_source, axis=1, keepdims=True).astype(jnp.int32)
    counts_ref[...] = jnp.broadcast_to(counts, counts_ref.shape)

    slot = lax.broadcasted_iota(jnp.int32, (1, total), 1)
    tile = divided(slot, slots)
    carried = jnp.concatenate(
        [
            tile.astype(jnp.float32), (slot - tile * slots).astype(jnp.float32), entry, owner,
            member, jnp.ones((1, total), jnp.float32),
        ],
        axis=0,
    ).astype(jnp.bfloat16)
    at = lax.broadcasted_iota(jnp.int32, (total, total), 0)
    for s in range(1, half):
        chosen = jnp.where(at == rank[s : s + 1], 1.0, 0.0).astype(jnp.bfloat16)
        listed = lax.dot_general(carried, chosen, NT, preferred_element_type=jnp.float32)
        listed = listed.astype(jnp.int32)
        lists_ref[3 * s - 3 : 3 * s - 2, :] = listed[0:1] * slots + listed[1:2]
        lists_ref[3 * s - 2 : 3 * s - 1, :] = listed[2:3]
        lists_ref[3 * s - 1 : 3 * s, :] = listed[0:1]
        target_ref[s - 1 : s, :] = jnp.where(listed[5:6] > 0, listed[3:4] * rows + listed[4:5], -1)

    index_ref[...] = jnp.full(index_ref.shape, -1.0, jnp.float32)
    groups = fetch_ref.shape[1] // per_peer
    for p in range(groups):
        part = within[:, p * per_peer : (p + 1) * per_peer].astype(jnp.float32)
        group = jnp.max(
            jnp.where(ghost_lane == p * per_peer, divided(fetched, group_size), 0)
        )
        index_ref[group, :, 0:per_peer] = part


def terms_of(parts, spread, lane_block):
    mode_count = parts[0][0].shape[0]
    halves = [[] for _ in range(mode_count // BATCH)]
    for b in range(len(parts) // BATCH):
        part = parts[b * BATCH : (b + 1) * BATCH]
        block = lax.dot_general(
            jnp.concatenate([s for s, _ in part], axis=0),
            jnp.concatenate([q for _, q in part[::-1]], axis=0),
            NT,
            preferred_element_type=jnp.float32,
        )
        for j in range(BATCH):
            for half in range(mode_count // BATCH):
                row = j * mode_count + half * BATCH
                value = pltpu.roll(block[row : row + BATCH], 0, 1, stride=mode_count, stride_axis=0)
                value = jnp.where(lane_block == BATCH - 1 - j, value, 0.0)
                halves[half].append(value)
    halves = [jnp.concatenate(h, axis=0).astype(jnp.bfloat16) for h in halves]
    flat = jnp.dot(spread, jnp.concatenate(halves, axis=1), preferred_element_type=jnp.float32)
    rows = []
    for b in range(len(parts) // BATCH):
        row = flat[b * BATCH : (b + 1) * BATCH]
        rows.append(
            jnp.concatenate(
                [
                    pltpu.roll(row[:, h * LANES : (h + 1) * LANES], mode_count, 1, stride=mode_count, stride_axis=0)
                    for h in range(len(halves))
                ],
                axis=1,
            )
        )
    return jnp.concatenate(rows, axis=0)


def term_constants(count, mode_count):
    spread = lax.broadcasted_iota(jnp.int32, (count, count * BATCH), 1) // BATCH
    spread = spread == lax.broadcasted_iota(jnp.int32, (count, count * BATCH), 0)
    lane_block = (
        lax.broadcasted_iota(jnp.int32, (BATCH, LANES), 1) // mode_count
        - lax.broadcasted_iota(jnp.int32, (BATCH, LANES), 0)
    ) & (BATCH - 1)
    return jnp.where(spread, 1.0, 0.0).astype(jnp.bfloat16), lane_block


def product_pair(picked, tiles):
    zero = jnp.zeros_like(picked[0])
    left = jnp.concatenate(
        [
            jnp.concatenate([picked[0], zero], axis=1),
            jnp.concatenate([zero, picked[1]], axis=1),
        ],
        axis=0,
    )
    right = jnp.concatenate(tiles, axis=1)
    both = lax.dot_general(left, right, NT, preferred_element_type=jnp.float32)
    rows = picked[0].shape[0]
    return both[:rows], both[rows:]


def own_kernel(
    slots, group_size, place, row_ref, table_ref, a_hbm,
    prolong_ref, weight_ref, sums_ref, far_ref, a_ref, product_ref, terms_ref, arrived,
):
    tile_dev = weight_ref.shape[0]
    mode_count, tile_rows = table_ref.shape[1:]
    pair = 2
    per_step = pair * slots
    steps = tile_dev // pair
    diagonal = lax.broadcasted_iota(jnp.int32, (tile_rows, tile_rows), 0) == lax.broadcasted_iota(
        jnp.int32, (tile_rows, tile_rows), 1
    )
    spread, lane_block = term_constants(per_step, mode_count)

    def fetch(step):
        part = pl.ds(step * per_step, per_step)
        return pltpu.make_async_copy(a_hbm.at[part], a_ref.at[part], arrived.at[step])

    @pl.loop(0, steps)
    def _(step):
        fetch(step).start()

    def finish(step):
        first = step * per_step
        parts = [(prolong_ref[first + k], product_ref[first + k]) for k in range(per_step)]
        terms_ref[pl.ds(pl.multiple_of(first, 8), per_step), :] = terms_of(parts, spread, lane_block)

    def begin(step):
        for i in range(pair):
            tile = step * pair + i
            lead = a_ref[tile * slots].astype(jnp.float32)
            entries = jnp.sum(jnp.where(diagonal, lead, 0.0), axis=0, keepdims=True)
            weight = damping * (1.0 / entries)
            weight_ref[pl.ds(tile, 1), :] = weight
            for k in range(0, slots, 2):
                slot = tile * slots + k
                picked = [table_ref[place[slot]], table_ref[place[slot + 1]]]
                products = product_pair(picked, [a_ref[slot], a_ref[slot + 1]])
                for d, product in enumerate(products):
                    smooth = -(weight * product)
                    if k + d == 0:
                        smooth = picked[0].astype(jnp.float32) + smooth
                    prolong_ref[slot + d] = smooth.astype(jnp.bfloat16)
                    product_ref[slot + d] = product.astype(jnp.bfloat16)

    fetch(0).wait()
    begin(0)

    @pl.loop(1, steps)
    def _(step):
        fetch(step).wait()
        finish(step - 1)
        begin(step)

    finish(steps - 1)

    total = tile_dev * slots
    height = group_size + far_ref.shape[0]
    one_hot = lax.broadcasted_iota(jnp.int32, (height, total), 0) == row_ref[...]
    one_hot = jnp.where(one_hot, 1.0, 0.0).astype(jnp.bfloat16)
    sums = jnp.dot(one_hot, terms_ref[...].astype(jnp.bfloat16), preferred_element_type=jnp.float32)
    sums = sums * (1.0 / tile_rows)
    sums_ref[...] = sums[:group_size].astype(jnp.bfloat16)
    far_ref[...] = sums[group_size:]


def ghost_kernel(
    pitch, half, here, lists_ref, counts_ref, target_ref, index_ref, far_ref, a_ref, weight_ref, old_ref,
    *refs,
):
    sources = refs[:-5]
    prolong_ref, out_ref, smooth_ref, product_ref, terms_ref = refs[-5:]
    mode_count, tile_rows = sources[0].shape[1:]
    groups, copies, rows, width = out_ref.shape
    total = a_ref.shape[0]
    batch = 2 * BATCH
    spread, lane_block = term_constants(batch, mode_count)
    terms_ref[...] = jnp.zeros_like(terms_ref)
    result = jnp.zeros((groups * rows, width), jnp.float32)

    for s, table_ref in enumerate(sources):
        count = counts_ref[s + 1, 0]
        steps = (count + batch - 1) // batch

        def begin(step):
            for i in range(0, batch, 2):
                at = [jnp.minimum(step * batch + i + d, count - 1) for d in range(2)]
                slot = [lists_ref[3 * s, a] for a in at]
                picked = [table_ref[lists_ref[3 * s + 1, a]] for a in at]
                products = product_pair(picked, [a_ref[f] for f in slot])
                for d, product in enumerate(products):
                    weight = weight_ref[pl.ds(lists_ref[3 * s + 2, at[d]], 1), :]
                    smooth = (-(weight * product)).astype(jnp.bfloat16)
                    prolong_ref[slot[d]] = smooth
                    smooth_ref[i + d] = smooth
                    product_ref[i + d] = product.astype(jnp.bfloat16)

        def finish(step):
            parts = [(smooth_ref[i], product_ref[i]) for i in range(batch)]
            row = pl.multiple_of(step * batch, batch)
            terms_ref[pl.ds(row, batch), :] = terms_of(parts, spread, lane_block)

        @pl.when(count > 0)
        def _():
            begin(0)

            @pl.loop(1, steps)
            def _(step):
                finish(step - 1)
                begin(step)

            finish(steps - 1)

        one_hot = (
            lax.broadcasted_iota(jnp.int32, (groups * rows, total), 0) == target_ref[s : s + 1, :]
        )
        one_hot = jnp.where(one_hot, 1.0, 0.0).astype(jnp.bfloat16)
        result = result + jnp.dot(
            one_hot, terms_ref[0:total, :].astype(jnp.bfloat16), preferred_element_type=jnp.float32
        )

    result = (result * (1.0 / tile_rows)).reshape(groups, rows, width)
    row_place = lax.broadcasted_iota(jnp.int32, (groups, rows, width), 1)
    group_place = lax.broadcasted_iota(jnp.int32, (groups, rows, width), 0)
    result = jnp.where(group_place == (here[0] ^ half), far_ref[...][None], result)
    result = jnp.where(row_place == pitch, index_ref[...], result).astype(jnp.bfloat16)
    for copy in range(copies):
        out_ref[:, copy] = result


def target_kernel(pitch, incoming_ref, out_ref):
    senders, rows, width = incoming_ref.shape
    group_size = out_ref.shape[0]
    tile = lax.broadcasted_iota(jnp.int32, (group_size, rows), 0)
    total = jnp.zeros((group_size, width), jnp.float32)
    for sender in range(senders):
        value = incoming_ref[sender]
        wanted = value[pitch : pitch + 1, :rows].astype(jnp.float32).astype(jnp.int32)
        one_hot = (tile == wanted).astype(jnp.bfloat16)
        total = total + jnp.dot(one_hot, value, preferred_element_type=jnp.float32)
    out_ref[...] = total.astype(jnp.bfloat16)


def shards(a_tiles, modes, col_tiles, fetch_list):
    blk_count = lax.axis_size("blk")
    sub_count = lax.axis_size("sub")
    tile_dev, slot_count, tile_rows = a_tiles.shape[:3]
    mode_count = modes.shape[1]
    width = mode_count * mode_count
    group_size = tile_dev * blk_count
    ghost_count = fetch_list.shape[1]
    peer_count = min(NEIGHBOURS, sub_count - 1)
    per_peer = ghost_count // peer_count
    slot_total = tile_dev * slot_count
    half = sub_count // 2
    blk_half = blk_count // 2
    me = lax.axis_index("sub")
    lane = lax.axis_index("blk")

    far = xor_permute(modes, "sub", half)
    bits = []
    bit = blk_half
    own_part, far_part = modes[None], far[None]
    while bit:
        own_part = jnp.concatenate([own_part, xor_permute(own_part, "blk", bit)], axis=0)
        far_part = jnp.concatenate([far_part, xor_permute(far_part, "blk", bit)], axis=0)
        bits.append(bit)
        bit //= 2
    blank = jnp.zeros((1, mode_count, tile_rows), modes.dtype)
    table = jnp.concatenate(
        [
            own_part.reshape(group_size, mode_count, tile_rows),
            far_part.reshape(group_size, mode_count, tile_rows),
            blank,
        ],
        axis=0,
    )

    theirs = jnp.concatenate([xor_permute(fetch_list, "sub", peer) for peer in range(1, half)], axis=0)
    owners = theirs // group_size
    places = table_place(theirs % group_size, lane, tile_dev, bits)
    places = places + jnp.where(owners == (me ^ half), group_size, 0)
    here = jnp.stack([me, lane]).astype(jnp.int32)
    picks = pl.pallas_call(
        functools.partial(pick_kernel, per_peer, half),
        out_shape=[jax.ShapeDtypeStruct((2 * per_peer, mode_count, tile_rows), modes.dtype)] * (half - 1),
        in_specs=[SMEM, SMEM, SMEM, VMEM],
        out_specs=[VMEM] * (half - 1),
        name="pick",
        compiler_params=PARAMS,
    )(here, owners[:, ::per_peer], places, table)
    received = [xor_permute(picks[peer - 1], "sub", peer) for peer in range(1, half)]

    rows = -(-(per_peer + 1) // 8) * 8
    place, own_row, lists, counts, target, index_rows = pl.pallas_call(
        functools.partial(prep_kernel, slot_count, tile_dev, per_peer, rows, half, tuple(bits)),
        out_shape=[
            jax.ShapeDtypeStruct((1, slot_total), jnp.int32),
            jax.ShapeDtypeStruct((1, slot_total), jnp.int32),
            jax.ShapeDtypeStruct((3 * (half - 1), slot_total), jnp.int32),
            jax.ShapeDtypeStruct((-(-half // 8) * 8, LANES), jnp.int32),
            jax.ShapeDtypeStruct((half - 1, slot_total), jnp.int32),
            jax.ShapeDtypeStruct((sub_count, 1, width), jnp.float32),
        ],
        in_specs=[SMEM, VMEM, VMEM],
        out_specs=[VMEM] * 6,
        name="prep",
        compiler_params=PARAMS,
    )(here, col_tiles.reshape(1, slot_total), fetch_list)

    tiles = a_tiles.reshape(slot_total, tile_rows, tile_rows)
    tiles = pltpu.with_memory_space_constraint(tiles, pltpu.HBM)
    prolong, weight, own_sums, far_sums, tiles = pl.pallas_call(
        functools.partial(own_kernel, slot_count, group_size),
        out_shape=[
            pltpu.VMEM((slot_total, mode_count, tile_rows), jnp.bfloat16),
            jax.ShapeDtypeStruct((tile_dev, tile_rows), jnp.float32),
            jax.ShapeDtypeStruct((group_size, width), jnp.bfloat16),
            jax.ShapeDtypeStruct((rows, width), jnp.float32),
            pltpu.VMEM((slot_total, tile_rows, tile_rows), jnp.bfloat16),
        ],
        in_specs=[SMEM, VMEM, VMEM, pl.BlockSpec(memory_space=pltpu.HBM)],
        out_specs=[VMEM] * 5,
        scratch_shapes=[
            pltpu.VMEM((slot_total, mode_count, tile_rows), jnp.bfloat16),
            pltpu.VMEM((slot_total, width), jnp.float32),
            pltpu.SemaphoreType.DMA((tile_dev // 2,)),
        ],
        name="own",
        compiler_params=PARAMS,
    )(place.reshape(slot_total), own_row, table, tiles)

    prolong = pltpu.with_memory_space_constraint(prolong, pltpu.VMEM)
    tiles = pltpu.with_memory_space_constraint(tiles, pltpu.VMEM)
    own_total = own_sums
    bit = blk_half
    while bit:
        other = xor_permute(own_total, "blk", bit)
        own_total = own_total.astype(jnp.float32) + other.astype(jnp.float32)
        bit //= 2
        if bit:
            own_total = own_total.astype(jnp.bfloat16)

    prolong, outgoing = pl.pallas_call(
        functools.partial(ghost_kernel, per_peer, half),
        out_shape=[
            pltpu.VMEM((slot_total, mode_count, tile_rows), jnp.bfloat16),
            jax.ShapeDtypeStruct((sub_count, blk_half, rows, width), jnp.bfloat16),
        ],
        in_specs=[SMEM] * 3 + [VMEM] * (6 + half - 1),
        out_specs=[VMEM, VMEM],
        input_output_aliases={8: 0},
        scratch_shapes=[
            pltpu.VMEM((2 * BATCH, mode_count, tile_rows), jnp.bfloat16),
            pltpu.VMEM((2 * BATCH, mode_count, tile_rows), jnp.bfloat16),
            pltpu.VMEM((slot_total + 2 * BATCH, width), jnp.float32),
        ],
        name="ghost",
        compiler_params=PARAMS,
    )(here, lists, counts, target, index_rows, far_sums, tiles, weight, prolong, *received)

    groups = [
        [s * blk_count + high * 2 + core for s in range(sub_count) for high in range(blk_half)]
        for core in range(2)
    ]
    incoming = lax.all_to_all(
        outgoing.reshape(sub_count * blk_half, rows, width),
        ("sub", "blk"), split_axis=0, concat_axis=0, axis_index_groups=groups, tiled=True,
    )
    arrived = pl.pallas_call(
        functools.partial(target_kernel, per_peer),
        out_shape=jax.ShapeDtypeStruct((group_size, width), jnp.bfloat16),
        in_specs=[VMEM],
        out_specs=VMEM,
        name="target",
        compiler_params=PARAMS,
    )(incoming)
    other = xor_permute(arrived, "blk", 1)
    coarse_diag = own_total + (arrived.astype(jnp.float32) + other.astype(jnp.float32))
    return prolong.reshape(tile_dev, slot_count, mode_count, tile_rows), coarse_diag


def solution(mesh):
    in_specs = (
        P(("sub", "blk"), None, None, None),
        P(("sub", "blk"), None, None),
        P(("sub", "blk"), None),
        P(("sub", "blk"), None),
    )
    out_specs = (P(("sub", "blk"), None, None, None), P("sub", None))
    return jax.shard_map(shards, mesh=mesh, in_specs=in_specs, out_specs=out_specs, check_vma=False)
```

```python
import functools

import jax
import jax.numpy as jnp
from jax import lax
from jax.experimental import pallas as pl
from jax.experimental.pallas import tpu as pltpu
from jax.sharding import PartitionSpec as P


NEIGHBOURS = 26
LANES = 128
BATCH = 8

damping = 2.0 / 3.0

VMEM = pl.BlockSpec(memory_space=pltpu.VMEM)
SMEM = pl.BlockSpec(memory_space=pltpu.SMEM)
PARAMS = pltpu.CompilerParams(vmem_limit_bytes=8 << 20)
NT = (((1,), (1,)), ((), ()))


def xor_permute(x, axis, bit):
    count = lax.axis_size(axis)
    return lax.ppermute(x, axis, [(i, i ^ bit) for i in range(count)])


def divided(value, by):
    return jnp.floor((value.astype(jnp.float32) + 0.5) * (1.0 / by)).astype(jnp.int32)


def table_place(within, lane, tile_dev, bits):
    relative = divided(within, tile_dev)
    rest = within - relative * tile_dev
    relative = relative ^ lane
    order = jnp.zeros_like(relative)
    for i, bit in enumerate(bits):
        order = order + jnp.where((relative & bit) != 0, 1 << i, 0)
    return order * tile_dev + rest


def pick_kernel(count, half, here, owner_ref, place_ref, table_ref, *out_refs):
    for peer, out_ref in enumerate(out_refs):
        near = away = 0
        for p in range(owner_ref.shape[1]):
            owner = owner_ref[peer, p]
            near = jnp.where(owner == here[0], p * count, near)
            away = jnp.where(owner == here[0] ^ half, p * count, away)

        @pl.loop(0, count, unroll=2)
        def _(i):
            out_ref[i] = table_ref[place_ref[peer, near + i]]
            out_ref[count + i] = table_ref[place_ref[peer, away + i]]


def prep_kernel(
    slots, tile_dev, per_peer, rows, half, bits, here,
    cols_ref, fetch_ref, place_ref, row_ref, lists_ref, counts_ref, target_ref, index_ref,
):
    me, lane = here[0], here[1]
    total, ghosts = cols_ref.shape[1], fetch_ref.shape[1]
    group_size = tile_dev * (2 ** len(bits))
    fetched = fetch_ref[...]
    owner = divided(fetched, group_size)
    within = fetched - owner * group_size
    apart = owner ^ me
    low = apart & (half - 1)
    ghost_lane = lax.broadcasted_iota(jnp.int32, (1, ghosts), 1)
    member = ghost_lane - divided(ghost_lane, per_peer) * per_peer
    entry = jnp.where(
        low == 0,
        table_place(within, lane, tile_dev, bits),
        jnp.where(apart >= half, per_peer, 0) + member,
    )
    known = jnp.concatenate([low, entry, owner, member], axis=0).astype(jnp.float32)
    known = known.astype(jnp.bfloat16)
    cols = cols_ref[...]
    match = lax.broadcasted_iota(jnp.int32, (ghosts, total), 0) == cols - group_size
    match = jnp.where(match, 1.0, 0.0).astype(jnp.bfloat16)
    found = jnp.dot(known, match, preferred_element_type=jnp.float32)
    low, entry, owner, member = (found[i : i + 1] for i in range(4))
    is_ghost = cols >= group_size
    source = jnp.where(is_ghost, low.astype(jnp.int32), -1)
    entry_int = entry.astype(jnp.int32)
    place_ref[...] = jnp.where(
        source < 0,
        table_place(cols, lane, tile_dev, bits),
        jnp.where(source == 0, group_size + entry_int, 2 * group_size),
    )
    row_ref[...] = jnp.where(source < 0, cols, -1)

    kind = lax.broadcasted_iota(jnp.int32, (8, total), 0)
    chosen = jnp.where(source > 0, 1, source)
    by_kind = jnp.where(kind == chosen, 1.0, 0.0)
    before = lax.broadcasted_iota(jnp.int32, (total, total), 0) < lax.broadcasted_iota(
        jnp.int32, (total, total), 1
    )
    before = jnp.where(before, 1.0, 0.0).astype(jnp.bfloat16)
    rank = jnp.dot(by_kind.astype(jnp.bfloat16), before, preferred_element_type=jnp.float32)
    rank = jnp.where(by_kind > 0.5, rank, -1.0).astype(jnp.int32)
    counts = jnp.sum(by_kind, axis=1, keepdims=True).astype(jnp.int32)
    counts_ref[...] = jnp.broadcast_to(counts, counts_ref.shape)

    slot = lax.broadcasted_iota(jnp.int32, (1, total), 1)
    tile = divided(slot, slots)
    carried = jnp.concatenate(
        [
            tile.astype(jnp.float32), (slot - tile * slots).astype(jnp.float32), entry, owner,
            member, low,
        ],
        axis=0,
    ).astype(jnp.bfloat16)
    at = lax.broadcasted_iota(jnp.int32, (total, total), 0)
    for which in range(2):
        count = counts[which : which + 1]
        wanted = jnp.where(at < count, at, 0)
        chosen = jnp.where(wanted == rank[which : which + 1], 1.0, 0.0).astype(jnp.bfloat16)
        listed = lax.dot_general(carried, chosen, NT, preferred_element_type=jnp.float32)
        listed = listed.astype(jnp.int32)
        base = 3 * which
        lists_ref[base : base + 1, :] = listed[0:1] * slots + listed[1:2]
        lists_ref[base + 1 : base + 2, :] = listed[2:3] + (listed[5:6] - 1) * (2 * per_peer)
        lists_ref[base + 2 : base + 3, :] = listed[0:1]
        row = listed[4:5] if which == 0 else listed[3:4] * rows + listed[4:5]
        target_ref[which : which + 1, :] = jnp.where(slot < count, row, -1)

    index_ref[...] = jnp.full(index_ref.shape, -1.0, jnp.float32)
    groups = fetch_ref.shape[1] // per_peer
    for p in range(groups):
        part = within[:, p * per_peer : (p + 1) * per_peer].astype(jnp.float32)
        group = jnp.max(
            jnp.where(ghost_lane == p * per_peer, divided(fetched, group_size), 0)
        )
        index_ref[group, :, 0:per_peer] = part


def terms_of(parts, spread, lane_block):
    mode_count = parts[0][0].shape[0]
    halves = [[] for _ in range(mode_count // BATCH)]
    for b in range(len(parts) // BATCH):
        part = parts[b * BATCH : (b + 1) * BATCH]
        block = lax.dot_general(
            jnp.concatenate([s for s, _ in part], axis=0),
            jnp.concatenate([q for _, q in part[::-1]], axis=0),
            NT,
            preferred_element_type=jnp.float32,
        )
        for j in range(BATCH):
            for half in range(mode_count // BATCH):
                row = j * mode_count + half * BATCH
                value = pltpu.roll(block[row : row + BATCH], 0, 1, stride=mode_count, stride_axis=0)
                value = jnp.where(lane_block == BATCH - 1 - j, value, 0.0)
                halves[half].append(value)
    halves = [jnp.concatenate(h, axis=0).astype(jnp.bfloat16) for h in halves]
    flat = jnp.dot(spread, jnp.concatenate(halves, axis=1), preferred_element_type=jnp.float32)
    rows = []
    for b in range(len(parts) // BATCH):
        row = flat[b * BATCH : (b + 1) * BATCH]
        rows.append(
            jnp.concatenate(
                [
                    pltpu.roll(row[:, h * LANES : (h + 1) * LANES], mode_count, 1, stride=mode_count, stride_axis=0)
                    for h in range(len(halves))
                ],
                axis=1,
            )
        )
    return jnp.concatenate(rows, axis=0)


def term_constants(count, mode_count):
    spread = lax.broadcasted_iota(jnp.int32, (count, count * BATCH), 1) // BATCH
    spread = spread == lax.broadcasted_iota(jnp.int32, (count, count * BATCH), 0)
    lane_block = (
        lax.broadcasted_iota(jnp.int32, (BATCH, LANES), 1) // mode_count
        - lax.broadcasted_iota(jnp.int32, (BATCH, LANES), 0)
    ) & (BATCH - 1)
    return jnp.where(spread, 1.0, 0.0).astype(jnp.bfloat16), lane_block


def product_pair(picked, tiles):
    zero = jnp.zeros_like(picked[0])
    left = jnp.concatenate(
        [
            jnp.concatenate([picked[0], zero], axis=1),
            jnp.concatenate([zero, picked[1]], axis=1),
        ],
        axis=0,
    )
    right = jnp.concatenate(tiles, axis=1)
    both = lax.dot_general(left, right, NT, preferred_element_type=jnp.float32)
    rows = picked[0].shape[0]
    return both[:rows], both[rows:]


def summed(one_hot_rows, place, terms, tile_rows):
    one_hot = lax.broadcasted_iota(jnp.int32, (one_hot_rows, place.shape[1]), 0) == place
    one_hot = jnp.where(one_hot, 1.0, 0.0).astype(jnp.bfloat16)
    sums = jnp.dot(one_hot, terms.astype(jnp.bfloat16), preferred_element_type=jnp.float32)
    return sums * (1.0 / tile_rows)


def own_kernel(
    slots, place, lists_ref, counts_ref, target_ref, table_ref, a_hbm,
    prolong_ref, weight_ref, product_ref, far_ref, a_ref, terms_ref, arrived,
):
    tile_dev = weight_ref.shape[0]
    mode_count, tile_rows = table_ref.shape[1:]
    pair = 2
    per_step = pair * slots
    steps = tile_dev // pair
    batch = 2 * BATCH
    diagonal = lax.broadcasted_iota(jnp.int32, (tile_rows, tile_rows), 0) == lax.broadcasted_iota(
        jnp.int32, (tile_rows, tile_rows), 1
    )

    def fetch(step):
        part = pl.ds(step * per_step, per_step)
        return pltpu.make_async_copy(a_hbm.at[part], a_ref.at[part], arrived.at[step])

    @pl.loop(0, steps)
    def _(step):
        fetch(step).start()

    @pl.loop(0, steps)
    def _(step):
        fetch(step).wait()
        for i in range(pair):
            tile = step * pair + i
            lead = a_ref[tile * slots].astype(jnp.float32)
            entries = jnp.sum(jnp.where(diagonal, lead, 0.0), axis=0, keepdims=True)
            weight = damping * (1.0 / entries)
            weight_ref[pl.ds(tile, 1), :] = weight
            for k in range(0, slots, 2):
                slot = tile * slots + k
                picked = [table_ref[place[slot]], table_ref[place[slot + 1]]]
                products = product_pair(picked, [a_ref[slot], a_ref[slot + 1]])
                for d, product in enumerate(products):
                    smooth = -(weight * product)
                    if k + d == 0:
                        smooth = picked[0].astype(jnp.float32) + smooth
                    prolong_ref[slot + d] = smooth.astype(jnp.bfloat16)
                    product_ref[slot + d] = product.astype(jnp.bfloat16)

    spread, lane_block = term_constants(batch, mode_count)
    terms_ref[...] = jnp.zeros_like(terms_ref)

    @pl.loop(0, (counts_ref[0, 0] + batch - 1) // batch)
    def _(step):
        slot = [lists_ref[0, step * batch + i] for i in range(batch)]
        parts = [(prolong_ref[f], product_ref[f]) for f in slot]
        row = pl.multiple_of(step * batch, batch)
        terms_ref[pl.ds(row, batch), :] = terms_of(parts, spread, lane_block)

    total = tile_dev * slots
    far_ref[...] = summed(far_ref.shape[0], target_ref[0:1, :], terms_ref[0:total, :], tile_rows)


def terms_kernel(row_ref, prolong_ref, product_ref, sums_ref, terms_ref):
    total, mode_count, tile_rows = prolong_ref.shape
    per_step = 6 * BATCH
    spread, lane_block = term_constants(per_step, mode_count)

    @pl.loop(0, total // per_step)
    def _(step):
        first = step * per_step
        parts = [(prolong_ref[first + k], product_ref[first + k]) for k in range(per_step)]
        terms_ref[pl.ds(pl.multiple_of(first, BATCH), per_step), :] = terms_of(parts, spread, lane_block)

    sums = summed(sums_ref.shape[0], row_ref[...], terms_ref[...], tile_rows)
    sums_ref[...] = sums.astype(jnp.bfloat16)


def ghost_kernel(
    pitch, half, here, lists_ref, counts_ref, target_ref, index_ref, far_ref, a_ref, weight_ref,
    old_ref, *refs,
):
    received = refs[: half - 1]
    prolong_ref, out_ref, table_ref, smooth_ref, product_ref, terms_ref = refs[half - 1 :]
    mode_count, tile_rows = table_ref.shape[1:]
    for s, part_ref in enumerate(received):
        count = part_ref.shape[0]
        table_ref[s * count : (s + 1) * count] = part_ref[...]
    groups, copies, rows, width = out_ref.shape
    total = a_ref.shape[0]
    batch = 2 * BATCH
    spread, lane_block = term_constants(batch, mode_count)
    terms_ref[...] = jnp.zeros_like(terms_ref)
    count = counts_ref[1, 0]
    steps = (count + batch - 1) // batch

    def begin(step):
        first = step * batch
        for i in range(0, batch, 2):
            slot = [lists_ref[3, first + i + d] for d in range(2)]
            picked = [table_ref[lists_ref[4, first + i + d]] for d in range(2)]
            products = product_pair(picked, [a_ref[f] for f in slot])
            for d, product in enumerate(products):
                weight = weight_ref[pl.ds(lists_ref[5, first + i + d], 1), :]
                smooth = (-(weight * product)).astype(jnp.bfloat16)
                prolong_ref[slot[d]] = smooth
                smooth_ref[i + d] = smooth
                product_ref[i + d] = product.astype(jnp.bfloat16)

    def finish(step):
        parts = [(smooth_ref[i], product_ref[i]) for i in range(batch)]
        row = pl.multiple_of(step * batch, batch)
        terms_ref[pl.ds(row, batch), :] = terms_of(parts, spread, lane_block)

    @pl.when(count > 0)
    def _():
        begin(0)

        @pl.loop(1, steps)
        def _(step):
            finish(step - 1)
            begin(step)

        finish(steps - 1)

    result = summed(groups * rows, target_ref[1:2, :], terms_ref[0:total, :], tile_rows)
    result = result.reshape(groups, rows, width)
    row_place = lax.broadcasted_iota(jnp.int32, (groups, rows, width), 1)
    group_place = lax.broadcasted_iota(jnp.int32, (groups, rows, width), 0)
    result = jnp.where(group_place == (here[0] ^ half), far_ref[...][None], result)
    result = jnp.where(row_place == pitch, index_ref[...], result).astype(jnp.bfloat16)
    for copy in range(copies):
        out_ref[:, copy] = result


def target_kernel(pitch, incoming_ref, out_ref):
    senders, rows, width = incoming_ref.shape
    group_size = out_ref.shape[0]
    tile = lax.broadcasted_iota(jnp.int32, (group_size, rows), 0)
    total = jnp.zeros((group_size, width), jnp.float32)
    for sender in range(senders):
        value = incoming_ref[sender]
        wanted = value[pitch : pitch + 1, :rows].astype(jnp.float32).astype(jnp.int32)
        one_hot = (tile == wanted).astype(jnp.bfloat16)
        total = total + jnp.dot(one_hot, value, preferred_element_type=jnp.float32)
    out_ref[...] = total.astype(jnp.bfloat16)


def shards(a_tiles, modes, col_tiles, fetch_list):
    blk_count = lax.axis_size("blk")
    sub_count = lax.axis_size("sub")
    tile_dev, slot_count, tile_rows = a_tiles.shape[:3]
    mode_count = modes.shape[1]
    width = mode_count * mode_count
    group_size = tile_dev * blk_count
    ghost_count = fetch_list.shape[1]
    peer_count = min(NEIGHBOURS, sub_count - 1)
    per_peer = ghost_count // peer_count
    slot_total = tile_dev * slot_count
    half = sub_count // 2
    blk_half = blk_count // 2
    me = lax.axis_index("sub")
    lane = lax.axis_index("blk")

    far = xor_permute(modes, "sub", half)
    bits = []
    bit = blk_half
    own_part, far_part = [modes], [far]
    while bit:
        own_part = own_part + [xor_permute(part, "blk", bit) for part in own_part]
        far_part = far_part + [xor_permute(part, "blk", bit) for part in far_part]
        bits.append(bit)
        bit //= 2
    blank = jnp.zeros((1, mode_count, tile_rows), modes.dtype)
    table = jnp.concatenate(own_part + far_part + [blank], axis=0)

    theirs = []
    for peer in range(1, half):
        theirs.append(xor_permute(fetch_list, "sub", peer))
    theirs = jnp.concatenate(theirs, axis=0)
    owners = theirs // group_size
    places = table_place(theirs % group_size, lane, tile_dev, bits)
    places = places + jnp.where(owners == (me ^ half), group_size, 0)
    here = jnp.stack([me, lane]).astype(jnp.int32)
    picks = pl.pallas_call(
        functools.partial(pick_kernel, per_peer, half),
        out_shape=[jax.ShapeDtypeStruct((2 * per_peer, mode_count, tile_rows), modes.dtype)] * (half - 1),
        in_specs=[SMEM, SMEM, SMEM, VMEM],
        out_specs=[VMEM] * (half - 1),
        name="pick",
        compiler_params=PARAMS,
    )(here, owners[:, ::per_peer], places, table)
    received = []
    for peer in range(1, half):
        received.append(xor_permute(picks[peer - 1], "sub", peer))

    rows = -(-(per_peer + 1) // 8) * 8
    place, own_row, lists, counts, target, index_rows = pl.pallas_call(
        functools.partial(prep_kernel, slot_count, tile_dev, per_peer, rows, half, tuple(bits)),
        out_shape=[
            jax.ShapeDtypeStruct((1, slot_total), jnp.int32),
            jax.ShapeDtypeStruct((1, slot_total), jnp.int32),
            jax.ShapeDtypeStruct((6, slot_total), jnp.int32),
            jax.ShapeDtypeStruct((8, LANES), jnp.int32),
            jax.ShapeDtypeStruct((2, slot_total), jnp.int32),
            jax.ShapeDtypeStruct((sub_count, 1, width), jnp.float32),
        ],
        in_specs=[SMEM, VMEM, VMEM],
        out_specs=[VMEM] * 6,
        name="prep",
        compiler_params=PARAMS,
    )(here, col_tiles.reshape(1, slot_total), fetch_list)

    tiles = a_tiles.reshape(slot_total, tile_rows, tile_rows)
    tiles = pltpu.with_memory_space_constraint(tiles, pltpu.HBM)
    terms_scratch = pltpu.VMEM((slot_total + 2 * BATCH, width), jnp.float32)
    vectors = (slot_total, mode_count, tile_rows)
    prolong, weight, product, far_sums, tiles = pl.pallas_call(
        functools.partial(own_kernel, slot_count),
        out_shape=[
            pltpu.VMEM(vectors, jnp.bfloat16),
            jax.ShapeDtypeStruct((tile_dev, tile_rows), jnp.float32),
            pltpu.VMEM(vectors, jnp.bfloat16),
            jax.ShapeDtypeStruct((rows, width), jnp.float32),
            pltpu.VMEM((slot_total, tile_rows, tile_rows), jnp.bfloat16),
        ],
        in_specs=[SMEM, SMEM, SMEM, VMEM, VMEM, pl.BlockSpec(memory_space=pltpu.HBM)],
        out_specs=[VMEM] * 5,
        scratch_shapes=[terms_scratch, pltpu.SemaphoreType.DMA((tile_dev // 2,))],
        name="own",
        compiler_params=PARAMS,
    )(place.reshape(slot_total), lists, counts, target, table, tiles)

    prolong = pltpu.with_memory_space_constraint(prolong, pltpu.VMEM)
    product = pltpu.with_memory_space_constraint(product, pltpu.VMEM)
    tiles = pltpu.with_memory_space_constraint(tiles, pltpu.VMEM)
    prolong, outgoing = pl.pallas_call(
        functools.partial(ghost_kernel, per_peer, half),
        out_shape=[
            pltpu.VMEM(vectors, jnp.bfloat16),
            jax.ShapeDtypeStruct((sub_count, blk_half, rows, width), jnp.bfloat16),
        ],
        in_specs=[SMEM] * 3 + [VMEM] * (6 + half - 1),
        out_specs=[VMEM, VMEM],
        input_output_aliases={8: 0},
        scratch_shapes=[
            pltpu.VMEM((2 * per_peer * (half - 1), mode_count, tile_rows), jnp.bfloat16),
            pltpu.VMEM((2 * BATCH, mode_count, tile_rows), jnp.bfloat16),
            pltpu.VMEM((2 * BATCH, mode_count, tile_rows), jnp.bfloat16),
            terms_scratch,
        ],
        name="ghost",
        compiler_params=PARAMS,
    )(here, lists, counts, target, index_rows, far_sums, tiles, weight, prolong, *received)
    finished = pltpu.with_memory_space_constraint(prolong, pltpu.VMEM)

    groups = [
        [s * blk_count + high * 2 + core for s in range(sub_count) for high in range(blk_half)]
        for core in range(2)
    ]
    incoming = lax.all_to_all(
        outgoing.reshape(sub_count * blk_half, rows, width),
        ("sub", "blk"), split_axis=0, concat_axis=0, axis_index_groups=groups, tiled=True,
    )

    own_total = pl.pallas_call(
        terms_kernel,
        out_shape=jax.ShapeDtypeStruct((group_size, width), jnp.bfloat16),
        in_specs=[VMEM] * 3,
        out_specs=VMEM,
        scratch_shapes=[pltpu.VMEM((slot_total, width), jnp.float32)],
        name="terms",
        compiler_params=PARAMS,
    )(own_row, finished, product)
    bit = blk_half
    while bit:
        other = xor_permute(own_total, "blk", bit)
        own_total = own_total.astype(jnp.float32) + other.astype(jnp.float32)
        bit //= 2
        if bit:
            own_total = own_total.astype(jnp.bfloat16)
    arrived = pl.pallas_call(
        functools.partial(target_kernel, per_peer),
        out_shape=jax.ShapeDtypeStruct((group_size, width), jnp.bfloat16),
        in_specs=[VMEM],
        out_specs=VMEM,
        name="target",
        compiler_params=PARAMS,
    )(incoming)
    other = xor_permute(arrived, "blk", 1)
    coarse_diag = own_total + (arrived.astype(jnp.float32) + other.astype(jnp.float32))
    return prolong.reshape(tile_dev, slot_count, mode_count, tile_rows), coarse_diag


def solution(mesh):
    in_specs = (
        P(("sub", "blk"), None, None, None),
        P(("sub", "blk"), None, None),
        P(("sub", "blk"), None),
        P(("sub", "blk"), None),
    )
    out_specs = (P(("sub", "blk"), None, None, None), P("sub", None))

    return jax.shard_map(shards, mesh=mesh, in_specs=in_specs, out_specs=out_specs, check_vma=False)
```

```python
import functools

import jax
import jax.numpy as jnp
from jax import lax
from jax.experimental import pallas as pl
from jax.experimental.pallas import tpu as pltpu
from jax.sharding import PartitionSpec as P


NEIGHBOURS = 26
LANES = 128
BATCH = 8

damping = 2.0 / 3.0


VMEM = pl.BlockSpec(memory_space=pltpu.VMEM)
SMEM = pl.BlockSpec(memory_space=pltpu.SMEM)
PARAMS = pltpu.CompilerParams(vmem_limit_bytes=8 << 20)
NT = (((1,), (1,)), ((), ()))


def xor_permute(x, axis, bit):
    count = lax.axis_size(axis)
    return lax.ppermute(x, axis, [(i, i ^ bit) for i in range(count)])


def divided(value, by):
    return jnp.floor((value.astype(jnp.float32) + 0.5) * (1.0 / by)).astype(jnp.int32)


def table_place(within, lane, tile_dev, bits):
    relative = divided(within, tile_dev)
    rest = within - relative * tile_dev
    relative = relative ^ lane
    order = jnp.zeros_like(relative)
    for i, bit in enumerate(bits):
        order = order + jnp.where((relative & bit) != 0, 1 << i, 0)
    return order * tile_dev + rest


def pick_kernel(count, half, here, owner_ref, place_ref, table_ref, *out_refs):
    for peer, out_ref in enumerate(out_refs):
        near = away = 0
        for p in range(owner_ref.shape[1]):
            owner = owner_ref[peer, p]
            near = jnp.where(owner == here[0], p * count, near)
            away = jnp.where(owner == here[0] ^ half, p * count, away)

        @pl.loop(0, count, unroll=2)
        def _(i):
            out_ref[i] = table_ref[place_ref[peer, near + i]]
            out_ref[count + i] = table_ref[place_ref[peer, away + i]]


def prep_kernel(
    slots, tile_dev, per_peer, rows, half, bits, here,
    cols_ref, fetch_ref, place_ref, row_ref, far_slot_ref, slot_ref, entry_ref, tile_ref, counts_ref,
    target_ref, index_ref,
):
    me, lane = here[0], here[1]
    total, ghosts = cols_ref.shape[1], fetch_ref.shape[1]
    group_size = tile_dev * (2 ** len(bits))
    fetched = fetch_ref[...]
    owner = divided(fetched, group_size)
    within = fetched - owner * group_size
    apart = owner ^ me
    low = apart & (half - 1)
    ghost_lane = lax.broadcasted_iota(jnp.int32, (1, ghosts), 1)
    member = ghost_lane - divided(ghost_lane, per_peer) * per_peer
    entry = jnp.where(
        low == 0,
        table_place(within, lane, tile_dev, bits),
        jnp.where(apart >= half, per_peer, 0) + member,
    )
    known = jnp.concatenate([low, entry, owner, member], axis=0).astype(jnp.float32)
    known = known.astype(jnp.bfloat16)
    cols = cols_ref[...]
    match = lax.broadcasted_iota(jnp.int32, (ghosts, total), 0) == cols - group_size
    match = jnp.where(match, 1.0, 0.0).astype(jnp.bfloat16)
    found = jnp.dot(known, match, preferred_element_type=jnp.float32)
    low, entry, owner, member = (found[i : i + 1] for i in range(4))
    is_ghost = cols >= group_size
    source = jnp.where(is_ghost, low.astype(jnp.int32), -1)
    entry_int = entry.astype(jnp.int32)
    place_ref[...] = jnp.where(
        source < 0,
        table_place(cols, lane, tile_dev, bits),
        jnp.where(source == 0, group_size + entry_int, 2 * group_size),
    )
    row_ref[...] = jnp.where(source < 0, cols, -1)

    kind = lax.broadcasted_iota(jnp.int32, (8, total), 0)
    chosen = jnp.where(source > 0, 1, source)
    by_kind = jnp.where(kind == chosen, 1.0, 0.0)
    before = lax.broadcasted_iota(jnp.int32, (total, total), 0) < lax.broadcasted_iota(
        jnp.int32, (total, total), 1
    )
    before = jnp.where(before, 1.0, 0.0).astype(jnp.bfloat16)
    rank = jnp.dot(by_kind.astype(jnp.bfloat16), before, preferred_element_type=jnp.float32)
    rank = jnp.where(by_kind > 0.5, rank, -1.0).astype(jnp.int32)
    counts = jnp.sum(by_kind, axis=1, keepdims=True).astype(jnp.int32)
    counts_ref[...] = jnp.broadcast_to(counts, counts_ref.shape)

    slot = lax.broadcasted_iota(jnp.int32, (1, total), 1)
    tile = divided(slot, slots)
    carried = jnp.concatenate(
        [
            tile.astype(jnp.float32), (slot - tile * slots).astype(jnp.float32), entry, owner,
            member, low,
        ],
        axis=0,
    ).astype(jnp.bfloat16)
    at = lax.broadcasted_iota(jnp.int32, (total, total), 0)
    for which in range(2):
        count = counts[which : which + 1]
        wanted = jnp.where(at < count, at, 0)
        chosen = jnp.where(wanted == rank[which : which + 1], 1.0, 0.0).astype(jnp.bfloat16)
        listed = lax.dot_general(carried, chosen, NT, preferred_element_type=jnp.float32)
        listed = listed.astype(jnp.int32)
        (far_slot_ref, slot_ref)[which][...] = listed[0:1] * slots + listed[1:2]
        if which:
            entry_ref[...] = listed[2:3] + (listed[5:6] - 1) * (2 * per_peer)
            tile_ref[...] = listed[0:1]
        row = listed[4:5] if which == 0 else listed[3:4] * rows + listed[4:5]
        target_ref[which : which + 1, :] = jnp.where(slot < count, row, -1)

    index_ref[...] = jnp.full(index_ref.shape, -1.0, jnp.float32)
    groups = fetch_ref.shape[1] // per_peer
    for p in range(groups):
        part = within[:, p * per_peer : (p + 1) * per_peer].astype(jnp.float32)
        group = jnp.max(
            jnp.where(ghost_lane == p * per_peer, divided(fetched, group_size), 0)
        )
        index_ref[group, :, 0:per_peer] = part


def terms_of(parts, spread, lane_block):
    mode_count = parts[0][0].shape[0]
    halves = [[] for _ in range(mode_count // BATCH)]
    for b in range(len(parts) // BATCH):
        part = parts[b * BATCH : (b + 1) * BATCH]
        block = lax.dot_general(
            jnp.concatenate([s for s, _ in part], axis=0),
            jnp.concatenate([q for _, q in part[::-1]], axis=0),
            NT,
            preferred_element_type=jnp.float32,
        )
        for j in range(BATCH):
            for half in range(mode_count // BATCH):
                row = j * mode_count + half * BATCH
                value = pltpu.roll(block[row : row + BATCH], 0, 1, stride=mode_count, stride_axis=0)
                value = jnp.where(lane_block == BATCH - 1 - j, value, 0.0)
                halves[half].append(value)
    halves = [jnp.concatenate(h, axis=0).astype(jnp.bfloat16) for h in halves]
    flat = jnp.dot(spread, jnp.concatenate(halves, axis=1), preferred_element_type=jnp.float32)
    rows = []
    for b in range(len(parts) // BATCH):
        row = flat[b * BATCH : (b + 1) * BATCH]
        rows.append(
            jnp.concatenate(
                [
                    pltpu.roll(row[:, h * LANES : (h + 1) * LANES], mode_count, 1, stride=mode_count, stride_axis=0)
                    for h in range(len(halves))
                ],
                axis=1,
            )
        )
    return jnp.concatenate(rows, axis=0)


def term_constants(count, mode_count):
    spread = lax.broadcasted_iota(jnp.int32, (count, count * BATCH), 1) // BATCH
    spread = spread == lax.broadcasted_iota(jnp.int32, (count, count * BATCH), 0)
    lane_block = (
        lax.broadcasted_iota(jnp.int32, (BATCH, LANES), 1) // mode_count
        - lax.broadcasted_iota(jnp.int32, (BATCH, LANES), 0)
    ) & (BATCH - 1)
    return jnp.where(spread, 1.0, 0.0).astype(jnp.bfloat16), lane_block


def product_pair(picked, tiles):
    zero = jnp.zeros_like(picked[0])
    left = jnp.concatenate(
        [
            jnp.concatenate([picked[0], zero], axis=1),
            jnp.concatenate([zero, picked[1]], axis=1),
        ],
        axis=0,
    )
    right = jnp.concatenate(tiles, axis=1)
    both = lax.dot_general(left, right, NT, preferred_element_type=jnp.float32)
    rows = picked[0].shape[0]
    return both[:rows], both[rows:]


def summed(one_hot_rows, place, terms, tile_rows):
    one_hot = lax.broadcasted_iota(jnp.int32, (one_hot_rows, place.shape[1]), 0) == place
    one_hot = jnp.where(one_hot, 1.0, 0.0).astype(jnp.bfloat16)
    sums = jnp.dot(one_hot, terms.astype(jnp.bfloat16), preferred_element_type=jnp.float32)
    return sums * (1.0 / tile_rows)


def own_kernel(
    slots, place, far_slot, counts_ref, target_ref, table_ref, a_hbm,
    prolong_ref, weight_ref, product_ref, far_ref, a_ref, terms_ref, arrived,
):
    tile_dev = weight_ref.shape[0]
    mode_count, tile_rows = table_ref.shape[1:]
    pair = 4
    per_step = pair * slots
    steps = tile_dev // pair
    batch = 2 * BATCH
    diagonal = lax.broadcasted_iota(jnp.int32, (tile_rows, tile_rows), 0) == lax.broadcasted_iota(
        jnp.int32, (tile_rows, tile_rows), 1
    )

    def fetch(step):
        part = pl.ds(step * per_step, per_step)
        return pltpu.make_async_copy(a_hbm.at[part], a_ref.at[part], arrived.at[step])

    @pl.loop(0, steps)
    def _(step):
        fetch(step).start()

    @pl.loop(0, steps)
    def _(step):
        fetch(step).wait()
        for i in range(pair):
            tile = step * pair + i
            lead = a_ref[tile * slots].astype(jnp.float32)
            entries = jnp.sum(jnp.where(diagonal, lead, 0.0), axis=0, keepdims=True)
            weight = damping * (1.0 / entries)
            weight_ref[tile] = weight
            for k in range(0, slots, 2):
                slot = tile * slots + k
                picked = [table_ref[place[slot]], table_ref[place[slot + 1]]]
                products = product_pair(picked, [a_ref[slot], a_ref[slot + 1]])
                for d, product in enumerate(products):
                    smooth = -(weight * product)
                    if k + d == 0:
                        smooth = picked[0].astype(jnp.float32) + smooth
                    prolong_ref[slot + d] = smooth.astype(jnp.bfloat16)
                    product_ref[slot + d] = product.astype(jnp.bfloat16)

    spread, lane_block = term_constants(batch, mode_count)
    terms_ref[...] = jnp.zeros_like(terms_ref)

    @pl.loop(0, (counts_ref[0, 0] + batch - 1) // batch)
    def _(step):
        slot = [far_slot[step * batch + i] for i in range(batch)]
        parts = [(prolong_ref[f], product_ref[f]) for f in slot]
        row = pl.multiple_of(step * batch, batch)
        terms_ref[pl.ds(row, batch), :] = terms_of(parts, spread, lane_block)

    total = tile_dev * slots
    far_ref[...] = summed(far_ref.shape[0], target_ref[0:1, :], terms_ref[0:total, :], tile_rows)


def terms_kernel(row_ref, prolong_ref, product_ref, sums_ref, terms_ref):
    total, mode_count, tile_rows = prolong_ref.shape
    per_step = 6 * BATCH
    spread, lane_block = term_constants(per_step, mode_count)

    @pl.loop(0, total // per_step)
    def _(step):
        first = step * per_step
        parts = [(prolong_ref[first + k], product_ref[first + k]) for k in range(per_step)]
        terms_ref[pl.ds(pl.multiple_of(first, BATCH), per_step), :] = terms_of(parts, spread, lane_block)

    sums = summed(sums_ref.shape[0], row_ref[...], terms_ref[...], tile_rows)
    sums_ref[...] = sums.astype(jnp.bfloat16)


def ghost_kernel(
    pitch, half, here, slots, entries, tiles, counts_ref, target_ref, index_ref, far_ref, a_ref, weight_ref,
    old_ref, *refs,
):
    received = refs[: half - 1]
    prolong_ref, out_ref, table_ref, smooth_ref, product_ref, terms_ref = refs[half - 1 :]
    mode_count, tile_rows = table_ref.shape[1:]
    for s, part_ref in enumerate(received):
        count = part_ref.shape[0]
        table_ref[s * count : (s + 1) * count] = part_ref[...]
    groups, copies, rows, width = out_ref.shape
    total = a_ref.shape[0]
    batch = 2 * BATCH
    spread, lane_block = term_constants(batch, mode_count)
    terms_ref[...] = jnp.zeros_like(terms_ref)
    count = counts_ref[1, 0]
    steps = (count + batch - 1) // batch

    def begin(step):
        first = step * batch
        for i in range(0, batch, 2):
            slot = [slots[first + i + d] for d in range(2)]
            picked = [table_ref[entries[first + i + d]] for d in range(2)]
            products = product_pair(picked, [a_ref[f] for f in slot])
            for d, product in enumerate(products):
                weight = weight_ref[tiles[first + i + d]]
                smooth = (-(weight * product)).astype(jnp.bfloat16)
                prolong_ref[slot[d]] = smooth
                smooth_ref[i + d] = smooth
                product_ref[i + d] = product.astype(jnp.bfloat16)

    def finish(step):
        parts = [(smooth_ref[i], product_ref[i]) for i in range(batch)]
        row = pl.multiple_of(step * batch, batch)
        terms_ref[pl.ds(row, batch), :] = terms_of(parts, spread, lane_block)

    @pl.when(count > 0)
    def _():
        begin(0)

        @pl.loop(1, steps)
        def _(step):
            finish(step - 1)
            begin(step)

        finish(steps - 1)

    result = summed(groups * rows, target_ref[1:2, :], terms_ref[0:total, :], tile_rows)
    result = result.reshape(groups, rows, width)
    row_place = lax.broadcasted_iota(jnp.int32, (groups, rows, width), 1)
    group_place = lax.broadcasted_iota(jnp.int32, (groups, rows, width), 0)
    result = jnp.where(group_place == (here[0] ^ half), far_ref[...][None], result)
    result = jnp.where(row_place == pitch, index_ref[...], result).astype(jnp.bfloat16)
    for copy in range(copies):
        out_ref[:, copy] = result


def target_kernel(pitch, incoming_ref, out_ref):
    senders, rows, width = incoming_ref.shape
    group_size = out_ref.shape[0]
    tile = lax.broadcasted_iota(jnp.int32, (group_size, rows), 0)
    total = jnp.zeros((group_size, width), jnp.float32)
    for sender in range(senders):
        value = incoming_ref[sender]
        wanted = value[pitch : pitch + 1, :rows].astype(jnp.float32).astype(jnp.int32)
        one_hot = (tile == wanted).astype(jnp.bfloat16)
        total = total + jnp.dot(one_hot, value, preferred_element_type=jnp.float32)
    out_ref[...] = total.astype(jnp.bfloat16)


def shards(a_tiles, modes, col_tiles, fetch_list):
    blk_count = lax.axis_size("blk")
    sub_count = lax.axis_size("sub")
    tile_dev, slot_count, tile_rows = a_tiles.shape[:3]
    mode_count = modes.shape[1]
    width = mode_count * mode_count
    group_size = tile_dev * blk_count
    ghost_count = fetch_list.shape[1]
    peer_count = min(NEIGHBOURS, sub_count - 1)
    per_peer = ghost_count // peer_count
    slot_total = tile_dev * slot_count
    half = sub_count // 2
    blk_half = blk_count // 2
    me = lax.axis_index("sub")
    lane = lax.axis_index("blk")

    far = xor_permute(modes, "sub", half)
    bits = []
    bit = blk_half
    own_part, far_part = [modes], [far]
    while bit:
        own_part = own_part + [xor_permute(part, "blk", bit) for part in own_part]
        far_part = far_part + [xor_permute(part, "blk", bit) for part in far_part]
        bits.append(bit)
        bit //= 2
    blank = jnp.zeros((1, mode_count, tile_rows), modes.dtype)
    table = jnp.concatenate(own_part + far_part + [blank], axis=0)

    theirs = []
    for peer in range(1, half):
        theirs.append(xor_permute(fetch_list, "sub", peer))
    theirs = jnp.concatenate(theirs, axis=0)
    owners = theirs // group_size
    places = table_place(theirs % group_size, lane, tile_dev, bits)
    places = places + jnp.where(owners == (me ^ half), group_size, 0)
    here = jnp.stack([me, lane]).astype(jnp.int32)
    picks = pl.pallas_call(
        functools.partial(pick_kernel, per_peer, half),
        out_shape=[pltpu.VMEM((2 * per_peer, mode_count, tile_rows), modes.dtype)] * (half - 1),
        in_specs=[SMEM, SMEM, SMEM, VMEM],
        out_specs=[VMEM] * (half - 1),
        name="pick",
        compiler_params=PARAMS,
    )(here, owners[:, ::per_peer], places, table)
    received = []
    for peer in range(1, half):
        received.append(xor_permute(picks[peer - 1], "sub", peer))

    rows = -(-(per_peer + 1) // 8) * 8
    columns = col_tiles.reshape(1, slot_total)
    place, own_row, far_slot, slot, entry, tile, counts, target, index_rows = pl.pallas_call(
        functools.partial(prep_kernel, slot_count, tile_dev, per_peer, rows, half, tuple(bits)),
        out_shape=[
            *[jax.ShapeDtypeStruct((1, slot_total), jnp.int32)] * 6,
            jax.ShapeDtypeStruct((8, LANES), jnp.int32),
            jax.ShapeDtypeStruct((2, slot_total), jnp.int32),
            jax.ShapeDtypeStruct((sub_count, 1, width), jnp.float32),
        ],
        in_specs=[SMEM, VMEM, VMEM],
        out_specs=[VMEM] * 9,
        name="prep",
        compiler_params=PARAMS,
    )(here, columns, fetch_list)

    tiles = a_tiles.reshape(slot_total, tile_rows, tile_rows)
    tiles = pltpu.with_memory_space_constraint(tiles, pltpu.HBM)
    terms_scratch = pltpu.VMEM((slot_total + 2 * BATCH, width), jnp.float32)
    vectors = (slot_total, mode_count, tile_rows)
    prolong, weight, product, far_sums, tiles = pl.pallas_call(
        functools.partial(own_kernel, slot_count),
        out_shape=[
            pltpu.VMEM(vectors, jnp.bfloat16),
            jax.ShapeDtypeStruct((tile_dev, 1, tile_rows), jnp.float32),
            pltpu.VMEM(vectors, jnp.bfloat16),
            jax.ShapeDtypeStruct((rows, width), jnp.float32),
            pltpu.VMEM((slot_total, tile_rows, tile_rows), jnp.bfloat16),
        ],
        in_specs=[SMEM, SMEM, SMEM, VMEM, VMEM, pl.BlockSpec(memory_space=pltpu.HBM)],
        out_specs=[VMEM] * 5,
        scratch_shapes=[terms_scratch, pltpu.SemaphoreType.DMA((tile_dev // 4,))],
        name="own",
        compiler_params=PARAMS,
    )(place.reshape(slot_total), far_slot.reshape(slot_total), counts, target, table, tiles)

    prolong = pltpu.with_memory_space_constraint(prolong, pltpu.VMEM)
    product = pltpu.with_memory_space_constraint(product, pltpu.VMEM)
    tiles = pltpu.with_memory_space_constraint(tiles, pltpu.VMEM)
    prolong, outgoing = pl.pallas_call(
        functools.partial(ghost_kernel, per_peer, half),
        out_shape=[
            pltpu.VMEM(vectors, jnp.bfloat16),
            jax.ShapeDtypeStruct((sub_count, blk_half, rows, width), jnp.bfloat16),
        ],
        in_specs=[SMEM] * 5 + [VMEM] * (6 + half - 1),
        out_specs=[VMEM, VMEM],
        input_output_aliases={10: 0},
        scratch_shapes=[
            pltpu.VMEM((2 * per_peer * (half - 1), mode_count, tile_rows), jnp.bfloat16),
            pltpu.VMEM((2 * BATCH, mode_count, tile_rows), jnp.bfloat16),
            pltpu.VMEM((2 * BATCH, mode_count, tile_rows), jnp.bfloat16),
            terms_scratch,
        ],
        name="ghost",
        compiler_params=PARAMS,
    )(
        here, slot.reshape(slot_total), entry.reshape(slot_total), tile.reshape(slot_total), counts,
        target, index_rows, far_sums, tiles, weight, prolong, *received,
    )
    finished = pltpu.with_memory_space_constraint(prolong, pltpu.VMEM)

    groups = [
        [s * blk_count + high * 2 + core for s in range(sub_count) for high in range(blk_half)]
        for core in range(2)
    ]
    incoming = lax.all_to_all(
        outgoing.reshape(sub_count * blk_half, rows, width),
        ("sub", "blk"), split_axis=0, concat_axis=0, axis_index_groups=groups, tiled=True,
    )

    own_total = pl.pallas_call(
        terms_kernel,
        out_shape=jax.ShapeDtypeStruct((group_size, width), jnp.bfloat16),
        in_specs=[VMEM] * 3,
        out_specs=VMEM,
        scratch_shapes=[pltpu.VMEM((slot_total, width), jnp.float32)],
        name="terms",
        compiler_params=PARAMS,
    )(own_row, finished, product)
    bit = blk_half
    while bit:
        other = xor_permute(own_total, "blk", bit)
        own_total = own_total.astype(jnp.float32) + other.astype(jnp.float32)
        bit //= 2
        if bit:
            own_total = own_total.astype(jnp.bfloat16)
    arrived = pl.pallas_call(
        functools.partial(target_kernel, per_peer),
        out_shape=jax.ShapeDtypeStruct((group_size, width), jnp.bfloat16),
        in_specs=[VMEM],
        out_specs=VMEM,
        name="target",
        compiler_params=PARAMS,
    )(incoming)
    other = xor_permute(arrived, "blk", 1)
    coarse_diag = own_total + (arrived.astype(jnp.float32) + other.astype(jnp.float32))
    return prolong.reshape(tile_dev, slot_count, mode_count, tile_rows), coarse_diag


def solution(mesh):
    in_specs = (
        P(("sub", "blk"), None, None, None),
        P(("sub", "blk"), None, None),
        P(("sub", "blk"), None),
        P(("sub", "blk"), None),
    )
    out_specs = (P(("sub", "blk"), None, None, None), P("sub", None))

    return jax.shard_map(shards, mesh=mesh, in_specs=in_specs, out_specs=out_specs, check_vma=False)
```

```python
import functools

import jax
import jax.numpy as jnp
from jax import lax
from jax.experimental import pallas as pl
from jax.experimental.pallas import tpu as pltpu
from jax.sharding import PartitionSpec as P


NEIGHBOURS = 26
LANES = 128
BATCH = 8

damping = 2.0 / 3.0


VMEM = pl.BlockSpec(memory_space=pltpu.VMEM)
SMEM = pl.BlockSpec(memory_space=pltpu.SMEM)
PARAMS = pltpu.CompilerParams(vmem_limit_bytes=8 << 20)
GHOST_PARAMS = pltpu.CompilerParams(vmem_limit_bytes=8 << 20)
NT = (((1,), (1,)), ((), ()))


def xor_permute(x, axis, bit):
    count = lax.axis_size(axis)
    return lax.ppermute(x, axis, [(i, i ^ bit) for i in range(count)])


def divided(value, by):
    return jnp.floor((value.astype(jnp.float32) + 0.5) * (1.0 / by)).astype(jnp.int32)


def table_place(within, lane, tile_dev, bits):
    relative = divided(within, tile_dev)
    rest = within - relative * tile_dev
    relative = relative ^ lane
    order = jnp.zeros_like(relative)
    for i, bit in enumerate(bits):
        order = order + jnp.where((relative & bit) != 0, 1 << i, 0)
    return order * tile_dev + rest


def pick_kernel(count, half, here, owner_ref, place_ref, table_ref, *out_refs):
    for peer, out_ref in enumerate(out_refs):
        near = away = 0
        for p in range(owner_ref.shape[1]):
            owner = owner_ref[peer, p]
            near = jnp.where(owner == here[0], p * count, near)
            away = jnp.where(owner == here[0] ^ half, p * count, away)

        @pl.loop(0, count, unroll=2)
        def _(i):
            out_ref[i] = table_ref[place_ref[peer, near + i]]
            out_ref[count + i] = table_ref[place_ref[peer, away + i]]


def prep_kernel(
    slots, tile_dev, per_peer, rows, half, bits, here,
    cols_ref, fetch_ref, place_ref, row_ref, far_slot_ref, slot_ref, entry_ref, tile_ref, counts_ref,
    target_ref, index_ref,
):
    me, lane = here[0], here[1]
    total, ghosts = cols_ref.shape[1], fetch_ref.shape[1]
    group_size = tile_dev * (2 ** len(bits))
    fetched = fetch_ref[...]
    owner = divided(fetched, group_size)
    within = fetched - owner * group_size
    apart = owner ^ me
    low = apart & (half - 1)
    ghost_lane = lax.broadcasted_iota(jnp.int32, (1, ghosts), 1)
    member = ghost_lane - divided(ghost_lane, per_peer) * per_peer
    entry = jnp.where(
        low == 0,
        table_place(within, lane, tile_dev, bits),
        jnp.where(apart >= half, per_peer, 0) + member,
    )
    known = jnp.concatenate([low, entry, owner, member], axis=0).astype(jnp.float32)
    known = known.astype(jnp.bfloat16)
    cols = cols_ref[...]
    match = lax.broadcasted_iota(jnp.int32, (ghosts, total), 0) == cols - group_size
    match = jnp.where(match, 1.0, 0.0).astype(jnp.bfloat16)
    found = jnp.dot(known, match, preferred_element_type=jnp.float32)
    low, entry, owner, member = (found[i : i + 1] for i in range(4))
    is_ghost = cols >= group_size
    source = jnp.where(is_ghost, low.astype(jnp.int32), -1)
    entry_int = entry.astype(jnp.int32)
    place_ref[...] = jnp.where(
        source < 0,
        table_place(cols, lane, tile_dev, bits),
        jnp.where(source == 0, group_size + entry_int, 2 * group_size),
    )[0]
    row_ref[...] = jnp.where(source < 0, cols, -1)

    kind = lax.broadcasted_iota(jnp.int32, (8, total), 0)
    chosen = jnp.where(source > 0, 1, source)
    by_kind = jnp.where(kind == chosen, 1.0, 0.0)
    before = lax.broadcasted_iota(jnp.int32, (total, total), 0) < lax.broadcasted_iota(
        jnp.int32, (total, total), 1
    )
    before = jnp.where(before, 1.0, 0.0).astype(jnp.bfloat16)
    rank = jnp.dot(by_kind.astype(jnp.bfloat16), before, preferred_element_type=jnp.float32)
    rank = jnp.where(by_kind > 0.5, rank, -1.0).astype(jnp.int32)
    counts = jnp.sum(by_kind, axis=1, keepdims=True).astype(jnp.int32)
    counts_ref[...] = jnp.broadcast_to(counts, counts_ref.shape)

    slot = lax.broadcasted_iota(jnp.int32, (1, total), 1)
    tile = divided(slot, slots)
    carried = jnp.concatenate(
        [
            tile.astype(jnp.float32), (slot - tile * slots).astype(jnp.float32), entry, owner,
            member, low,
        ],
        axis=0,
    ).astype(jnp.bfloat16)
    at = lax.broadcasted_iota(jnp.int32, (total, total), 0)
    for which in range(2):
        count = counts[which : which + 1]
        wanted = jnp.where(at < count, at, 0)
        chosen = jnp.where(wanted == rank[which : which + 1], 1.0, 0.0).astype(jnp.bfloat16)
        listed = lax.dot_general(carried, chosen, NT, preferred_element_type=jnp.float32)
        listed = listed.astype(jnp.int32)
        (far_slot_ref, slot_ref)[which][...] = (listed[0:1] * slots + listed[1:2])[0]
        if which:
            entry_ref[...] = (listed[2:3] + (listed[5:6] - 1) * (2 * per_peer))[0]
            tile_ref[...] = listed[0]
        row = listed[4:5] if which == 0 else listed[3:4] * rows + listed[4:5]
        target_ref[which : which + 1, :] = jnp.where(slot < count, row, -1)

    index_ref[...] = jnp.full(index_ref.shape, -1.0, jnp.float32)
    groups = fetch_ref.shape[1] // per_peer
    for p in range(groups):
        part = within[:, p * per_peer : (p + 1) * per_peer].astype(jnp.float32)
        group = jnp.max(
            jnp.where(ghost_lane == p * per_peer, divided(fetched, group_size), 0)
        )
        index_ref[group, :, 0:per_peer] = part


def terms_of(parts, spread, lane_block):
    mode_count = parts[0][0].shape[0]
    halves = [[] for _ in range(mode_count // BATCH)]
    for b in range(len(parts) // BATCH):
        part = parts[b * BATCH : (b + 1) * BATCH]
        block = lax.dot_general(
            jnp.concatenate([s for s, _ in part], axis=0),
            jnp.concatenate([q for _, q in part[::-1]], axis=0),
            NT,
            preferred_element_type=jnp.float32,
        )
        for j in range(BATCH):
            for half in range(mode_count // BATCH):
                row = j * mode_count + half * BATCH
                value = pltpu.roll(block[row : row + BATCH], 0, 1, stride=mode_count, stride_axis=0)
                value = jnp.where(lane_block == BATCH - 1 - j, value, 0.0)
                halves[half].append(value)
    halves = [jnp.concatenate(h, axis=0).astype(jnp.bfloat16) for h in halves]
    flat = jnp.dot(spread, jnp.concatenate(halves, axis=1), preferred_element_type=jnp.float32)
    rows = []
    for b in range(len(parts) // BATCH):
        row = flat[b * BATCH : (b + 1) * BATCH]
        rows.append(
            jnp.concatenate(
                [
                    pltpu.roll(row[:, h * LANES : (h + 1) * LANES], mode_count, 1, stride=mode_count, stride_axis=0)
                    for h in range(len(halves))
                ],
                axis=1,
            )
        )
    return jnp.concatenate(rows, axis=0)


def term_constants(count, mode_count):
    spread = lax.broadcasted_iota(jnp.int32, (count, count * BATCH), 1) // BATCH
    spread = spread == lax.broadcasted_iota(jnp.int32, (count, count * BATCH), 0)
    lane_block = (
        lax.broadcasted_iota(jnp.int32, (BATCH, LANES), 1) // mode_count
        - lax.broadcasted_iota(jnp.int32, (BATCH, LANES), 0)
    ) & (BATCH - 1)
    return jnp.where(spread, 1.0, 0.0).astype(jnp.bfloat16), lane_block


def product_pair(picked, tiles):
    zero = jnp.zeros_like(picked[0])
    left = jnp.concatenate(
        [
            jnp.concatenate([picked[0], zero], axis=1),
            jnp.concatenate([zero, picked[1]], axis=1),
        ],
        axis=0,
    )
    right = jnp.concatenate(tiles, axis=1)
    both = lax.dot_general(left, right, NT, preferred_element_type=jnp.float32)
    rows = picked[0].shape[0]
    return both[:rows], both[rows:]


def summed(one_hot_rows, place, terms, tile_rows):
    one_hot = lax.broadcasted_iota(jnp.int32, (one_hot_rows, place.shape[1]), 0) == place
    one_hot = jnp.where(one_hot, 1.0, 0.0).astype(jnp.bfloat16)
    sums = jnp.dot(one_hot, terms.astype(jnp.bfloat16), preferred_element_type=jnp.float32)
    return sums * (1.0 / tile_rows)


def own_kernel(
    slots, place, far_slot, counts_ref, target_ref, table_ref, a_hbm,
    prolong_ref, weight_ref, product_ref, far_ref, a_ref, terms_ref, arrived,
):
    tile_dev = weight_ref.shape[0]
    mode_count, tile_rows = table_ref.shape[1:]
    pair = 4
    per_step = pair * slots
    steps = tile_dev // pair
    batch = 2 * BATCH
    diagonal = lax.broadcasted_iota(jnp.int32, (tile_rows, tile_rows), 0) == lax.broadcasted_iota(
        jnp.int32, (tile_rows, tile_rows), 1
    )

    def fetch(step):
        part = pl.ds(step * per_step, per_step)
        return pltpu.make_async_copy(a_hbm.at[part], a_ref.at[part], arrived.at[step])

    @pl.loop(0, steps)
    def _(step):
        fetch(step).start()

    @pl.loop(0, steps)
    def _(step):
        fetch(step).wait()
        for i in range(pair):
            tile = step * pair + i
            lead = a_ref[tile * slots].astype(jnp.float32)
            entries = jnp.sum(jnp.where(diagonal, lead, 0.0), axis=0, keepdims=True)
            weight = damping * (1.0 / entries)
            weight_ref[tile] = weight
            for k in range(0, slots, 2):
                slot = tile * slots + k
                picked = [table_ref[place[slot]], table_ref[place[slot + 1]]]
                products = product_pair(picked, [a_ref[slot], a_ref[slot + 1]])
                for d, product in enumerate(products):
                    smooth = -(weight * product)
                    if k + d == 0:
                        smooth = picked[0].astype(jnp.float32) + smooth
                    prolong_ref[slot + d] = smooth.astype(jnp.bfloat16)
                    product_ref[slot + d] = product.astype(jnp.bfloat16)

    spread, lane_block = term_constants(batch, mode_count)
    terms_ref[...] = jnp.zeros_like(terms_ref)

    @pl.loop(0, (counts_ref[0, 0] + batch - 1) // batch)
    def _(step):
        slot = [far_slot[step * batch + i] for i in range(batch)]
        parts = [(prolong_ref[f], product_ref[f]) for f in slot]
        row = pl.multiple_of(step * batch, batch)
        terms_ref[pl.ds(row, batch), :] = terms_of(parts, spread, lane_block)

    total = tile_dev * slots
    far_ref[...] = summed(far_ref.shape[0], target_ref[0:1, :], terms_ref[0:total, :], tile_rows)


def terms_kernel(row_ref, prolong_ref, product_ref, sums_ref, terms_ref):
    total, mode_count, tile_rows = prolong_ref.shape
    per_step = 6 * BATCH
    spread, lane_block = term_constants(per_step, mode_count)

    @pl.loop(0, total // per_step)
    def _(step):
        first = step * per_step
        parts = [(prolong_ref[first + k], product_ref[first + k]) for k in range(per_step)]
        terms_ref[pl.ds(pl.multiple_of(first, BATCH), per_step), :] = terms_of(parts, spread, lane_block)

    sums = summed(sums_ref.shape[0], row_ref[...], terms_ref[...], tile_rows)
    sums_ref[...] = sums.astype(jnp.bfloat16)


def ghost_kernel(
    pitch, half, here, slots, entries, tiles, counts_ref, target_ref, index_ref, far_ref, a_ref, weight_ref,
    old_ref, *refs,
):
    received = refs[: half - 1]
    prolong_ref, out_ref, table_ref, smooth_ref, product_ref, terms_ref = refs[half - 1 :]
    mode_count, tile_rows = table_ref.shape[1:]
    for s, part_ref in enumerate(received):
        count = part_ref.shape[0]
        table_ref[s * count : (s + 1) * count] = part_ref[...]
    groups, copies, rows, width = out_ref.shape
    total = a_ref.shape[0]
    batch = 2 * BATCH
    spread, lane_block = term_constants(batch, mode_count)
    terms_ref[...] = jnp.zeros_like(terms_ref)
    count = counts_ref[1, 0]
    steps = (count + batch - 1) // batch

    def begin(step):
        first = step * batch
        for i in range(0, batch, 2):
            slot = [slots[first + i + d] for d in range(2)]
            picked = [table_ref[entries[first + i + d]] for d in range(2)]
            products = product_pair(picked, [a_ref[f] for f in slot])
            for d, product in enumerate(products):
                weight = weight_ref[tiles[first + i + d]]
                smooth = (-(weight * product)).astype(jnp.bfloat16)
                prolong_ref[slot[d]] = smooth
                smooth_ref[i + d] = smooth
                product_ref[i + d] = product.astype(jnp.bfloat16)

    def finish(step):
        parts = [(smooth_ref[i], product_ref[i]) for i in range(batch)]
        row = pl.multiple_of(step * batch, batch)
        terms_ref[pl.ds(row, batch), :] = terms_of(parts, spread, lane_block)

    begin(0)

    @pl.loop(1, steps)
    def _(step):
        finish(step - 1)
        begin(step)

    finish(steps - 1)
    result = summed(groups * rows, target_ref[1:2, :], terms_ref[0:total, :], tile_rows)
    result = result.reshape(groups, rows, width)
    row_place = lax.broadcasted_iota(jnp.int32, (groups, rows, width), 1)
    group_place = lax.broadcasted_iota(jnp.int32, (groups, rows, width), 0)
    result = jnp.where(group_place == (here[0] ^ half), far_ref[...][None], result)
    result = jnp.where(row_place == pitch, index_ref[...], result).astype(jnp.bfloat16)
    for copy in range(copies):
        out_ref[:, copy] = result


def target_kernel(pitch, incoming_ref, out_ref):
    senders, rows, width = incoming_ref.shape
    group_size = out_ref.shape[0]
    tile = lax.broadcasted_iota(jnp.int32, (group_size, rows), 0)
    total = jnp.zeros((group_size, width), jnp.float32)
    for sender in range(senders):
        value = incoming_ref[sender]
        wanted = value[pitch : pitch + 1, :rows].astype(jnp.float32).astype(jnp.int32)
        one_hot = (tile == wanted).astype(jnp.bfloat16)
        total = total + jnp.dot(one_hot, value, preferred_element_type=jnp.float32)
    out_ref[...] = total.astype(jnp.bfloat16)


def shards(a_tiles, modes, col_tiles, fetch_list):
    blk_count = lax.axis_size("blk")
    sub_count = lax.axis_size("sub")
    tile_dev, slot_count, tile_rows = a_tiles.shape[:3]
    mode_count = modes.shape[1]
    width = mode_count * mode_count
    group_size = tile_dev * blk_count
    ghost_count = fetch_list.shape[1]
    peer_count = min(NEIGHBOURS, sub_count - 1)
    per_peer = ghost_count // peer_count
    slot_total = tile_dev * slot_count
    half = sub_count // 2
    blk_half = blk_count // 2
    me = lax.axis_index("sub")
    lane = lax.axis_index("blk")

    far = xor_permute(modes, "sub", half)
    bits = []
    bit = blk_half
    own_part, far_part = [modes], [far]
    while bit:
        own_part = own_part + [xor_permute(part, "blk", bit) for part in own_part]
        far_part = far_part + [xor_permute(part, "blk", bit) for part in far_part]
        bits.append(bit)
        bit //= 2
    blank = jnp.zeros((1, mode_count, tile_rows), modes.dtype)
    table = jnp.concatenate(own_part + far_part + [blank], axis=0)

    theirs = []
    for peer in range(1, half):
        theirs.append(xor_permute(fetch_list, "sub", peer))
    theirs = jnp.concatenate(theirs, axis=0)
    owners = theirs // group_size
    places = table_place(theirs % group_size, lane, tile_dev, bits)
    places = places + jnp.where(owners == (me ^ half), group_size, 0)
    here = jnp.stack([me, lane]).astype(jnp.int32)
    picks = pl.pallas_call(
        functools.partial(pick_kernel, per_peer, half),
        out_shape=[jax.ShapeDtypeStruct((2 * per_peer, mode_count, tile_rows), modes.dtype)] * (half - 1),
        in_specs=[SMEM, SMEM, SMEM, VMEM],
        out_specs=[VMEM] * (half - 1),
        name="pick",
        compiler_params=PARAMS,
    )(here, owners[:, ::per_peer], places, table)
    received = []
    for peer in range(1, half):
        received.append(xor_permute(picks[peer - 1], "sub", peer))

    rows = -(-(per_peer + 1) // 8) * 8
    columns = col_tiles.reshape(1, slot_total)
    place, own_row, far_slot, slot, entry, tile, counts, target, index_rows = pl.pallas_call(
        functools.partial(prep_kernel, slot_count, tile_dev, per_peer, rows, half, tuple(bits)),
        out_shape=[
            jax.ShapeDtypeStruct((slot_total,), jnp.int32),
            jax.ShapeDtypeStruct((1, slot_total), jnp.int32),
            *[jax.ShapeDtypeStruct((slot_total,), jnp.int32)] * 4,
            jax.ShapeDtypeStruct((8, LANES), jnp.int32),
            jax.ShapeDtypeStruct((2, slot_total), jnp.int32),
            jax.ShapeDtypeStruct((sub_count, 1, width), jnp.float32),
        ],
        in_specs=[SMEM, VMEM, VMEM],
        out_specs=[VMEM] * 9,
        name="prep",
        compiler_params=PARAMS,
    )(here, columns, fetch_list)

    tiles = a_tiles.reshape(slot_total, tile_rows, tile_rows)
    tiles = pltpu.with_memory_space_constraint(tiles, pltpu.HBM)
    terms_scratch = pltpu.VMEM((slot_total + 2 * BATCH, width), jnp.float32)
    vectors = (slot_total, mode_count, tile_rows)
    prolong, weight, product, far_sums, tiles = pl.pallas_call(
        functools.partial(own_kernel, slot_count),
        out_shape=[
            pltpu.VMEM(vectors, jnp.bfloat16),
            jax.ShapeDtypeStruct((tile_dev, 1, tile_rows), jnp.float32),
            pltpu.VMEM(vectors, jnp.bfloat16),
            jax.ShapeDtypeStruct((rows, width), jnp.float32),
            pltpu.VMEM((slot_total, tile_rows, tile_rows), jnp.bfloat16),
        ],
        in_specs=[SMEM, SMEM, SMEM, VMEM, VMEM, pl.BlockSpec(memory_space=pltpu.HBM)],
        out_specs=[VMEM] * 5,
        scratch_shapes=[terms_scratch, pltpu.SemaphoreType.DMA((tile_dev // 4,))],
        name="own",
        compiler_params=PARAMS,
    )(place, far_slot, counts, target, table, tiles)

    prolong = pltpu.with_memory_space_constraint(prolong, pltpu.VMEM)
    product = pltpu.with_memory_space_constraint(product, pltpu.VMEM)
    tiles = pltpu.with_memory_space_constraint(tiles, pltpu.VMEM)
    prolong, outgoing = pl.pallas_call(
        functools.partial(ghost_kernel, per_peer, half),
        out_shape=[
            pltpu.VMEM(vectors, jnp.bfloat16),
            jax.ShapeDtypeStruct((sub_count, blk_half, rows, width), jnp.bfloat16),
        ],
        in_specs=[SMEM] * 5 + [VMEM] * (6 + half - 1),
        out_specs=[VMEM, VMEM],
        input_output_aliases={10: 0},
        scratch_shapes=[
            pltpu.VMEM((2 * per_peer * (half - 1), mode_count, tile_rows), jnp.bfloat16),
            pltpu.VMEM((2 * BATCH, mode_count, tile_rows), jnp.bfloat16),
            pltpu.VMEM((2 * BATCH, mode_count, tile_rows), jnp.bfloat16),
            terms_scratch,
        ],
        name="ghost",
        compiler_params=GHOST_PARAMS,
    )(
        here, slot, entry, tile, counts,
        target, index_rows, far_sums, tiles, weight, prolong, *received,
    )
    finished = pltpu.with_memory_space_constraint(prolong, pltpu.VMEM)

    groups = [
        [s * blk_count + high * 2 + core for s in range(sub_count) for high in range(blk_half)]
        for core in range(2)
    ]
    incoming = lax.all_to_all(
        outgoing.reshape(sub_count * blk_half, rows, width),
        ("sub", "blk"), split_axis=0, concat_axis=0, axis_index_groups=groups, tiled=True,
    )

    own_total = pl.pallas_call(
        terms_kernel,
        out_shape=jax.ShapeDtypeStruct((group_size, width), jnp.bfloat16),
        in_specs=[VMEM] * 3,
        out_specs=VMEM,
        scratch_shapes=[pltpu.VMEM((slot_total, width), jnp.float32)],
        name="terms",
        compiler_params=PARAMS,
    )(own_row, finished, product)
    bit = blk_half
    while bit:
        other = xor_permute(own_total, "blk", bit)
        own_total = own_total.astype(jnp.float32) + other.astype(jnp.float32)
        bit //= 2
        if bit:
            own_total = own_total.astype(jnp.bfloat16)
    arrived = pl.pallas_call(
        functools.partial(target_kernel, per_peer),
        out_shape=jax.ShapeDtypeStruct((group_size, width), jnp.bfloat16),
        in_specs=[VMEM],
        out_specs=VMEM,
        name="target",
        compiler_params=PARAMS,
    )(incoming)
    other = xor_permute(arrived, "blk", 1)
    coarse_diag = own_total + (arrived.astype(jnp.float32) + other.astype(jnp.float32))
    return prolong.reshape(tile_dev, slot_count, mode_count, tile_rows), coarse_diag


def solution(mesh):
    in_specs = (
        P(("sub", "blk"), None, None, None),
        P(("sub", "blk"), None, None),
        P(("sub", "blk"), None),
        P(("sub", "blk"), None),
    )
    out_specs = (P(("sub", "blk"), None, None, None), P("sub", None))

    return jax.shard_map(shards, mesh=mesh, in_specs=in_specs, out_specs=out_specs, check_vma=False)
```

```python
import functools

import jax
import jax.numpy as jnp
from jax import lax
from jax.experimental import pallas as pl
from jax.experimental.pallas import tpu as pltpu
from jax.sharding import PartitionSpec as P


NEIGHBOURS = 26
LANES = 128
BATCH = 8

damping = 2.0 / 3.0


VMEM = pl.BlockSpec(memory_space=pltpu.VMEM)
SMEM = pl.BlockSpec(memory_space=pltpu.SMEM)
PARAMS = pltpu.CompilerParams(vmem_limit_bytes=8 << 20)
GHOST_PARAMS = pltpu.CompilerParams(vmem_limit_bytes=8 << 20)
NT = (((1,), (1,)), ((), ()))


def xor_permute(x, axis, bit):
    count = lax.axis_size(axis)
    return lax.ppermute(x, axis, [(i, i ^ bit) for i in range(count)])


def divided(value, by):
    return jnp.floor((value.astype(jnp.float32) + 0.5) * (1.0 / by)).astype(jnp.int32)


def table_place(within, lane, tile_dev, bits):
    relative = divided(within, tile_dev)
    rest = within - relative * tile_dev
    relative = relative ^ lane
    order = jnp.zeros_like(relative)
    for i, bit in enumerate(bits):
        order = order + jnp.where((relative & bit) != 0, 1 << i, 0)
    return order * tile_dev + rest


def pick_kernel(count, half, here, owner_ref, place_ref, table_ref, *out_refs):
    for peer, out_ref in enumerate(out_refs):
        near = away = 0
        for p in range(owner_ref.shape[1]):
            owner = owner_ref[peer, p]
            near = jnp.where(owner == here[0], p * count, near)
            away = jnp.where(owner == here[0] ^ half, p * count, away)

        @pl.loop(0, count, unroll=2)
        def _(i):
            out_ref[i] = table_ref[place_ref[peer, near + i]]
            out_ref[count + i] = table_ref[place_ref[peer, away + i]]


def prep_kernel(
    slots, tile_dev, per_peer, rows, half, bits, here,
    cols_ref, fetch_ref, place_ref, row_ref, far_slot_ref, slot_ref, own_slot_ref, entry_ref, tile_ref, counts_ref,
    target_ref, index_ref,
):
    me, lane = here[0], here[1]
    total, ghosts = cols_ref.shape[1], fetch_ref.shape[1]
    group_size = tile_dev * (2 ** len(bits))
    fetched = fetch_ref[...]
    owner = divided(fetched, group_size)
    within = fetched - owner * group_size
    apart = owner ^ me
    low = apart & (half - 1)
    ghost_lane = lax.broadcasted_iota(jnp.int32, (1, ghosts), 1)
    member = ghost_lane - divided(ghost_lane, per_peer) * per_peer
    entry = jnp.where(
        low == 0,
        table_place(within, lane, tile_dev, bits),
        jnp.where(apart >= half, per_peer, 0) + member,
    )
    known = jnp.concatenate([low, entry, owner, member], axis=0).astype(jnp.float32)
    known = known.astype(jnp.bfloat16)
    cols = cols_ref[...]
    match = lax.broadcasted_iota(jnp.int32, (ghosts, total), 0) == cols - group_size
    match = jnp.where(match, 1.0, 0.0).astype(jnp.bfloat16)
    found = jnp.dot(known, match, preferred_element_type=jnp.float32)
    low, entry, owner, member = (found[i : i + 1] for i in range(4))
    is_ghost = cols >= group_size
    source = jnp.where(is_ghost, low.astype(jnp.int32), -1)
    entry_int = entry.astype(jnp.int32)
    place_ref[...] = jnp.where(
        source < 0,
        table_place(cols, lane, tile_dev, bits),
        jnp.where(source == 0, group_size + entry_int, 2 * group_size),
    )[0]

    kind = lax.broadcasted_iota(jnp.int32, (8, total), 0)
    chosen = jnp.where(source > 0, 1, jnp.where(source == 0, 0, 2))
    by_kind = jnp.where(kind == chosen, 1.0, 0.0)
    before = lax.broadcasted_iota(jnp.int32, (total, total), 0) < lax.broadcasted_iota(
        jnp.int32, (total, total), 1
    )
    before = jnp.where(before, 1.0, 0.0).astype(jnp.bfloat16)
    rank = jnp.dot(by_kind.astype(jnp.bfloat16), before, preferred_element_type=jnp.float32)
    rank = jnp.where(by_kind > 0.5, rank, -1.0).astype(jnp.int32)
    counts = jnp.sum(by_kind, axis=1, keepdims=True).astype(jnp.int32)
    counts_ref[...] = jnp.broadcast_to(counts, counts_ref.shape)

    slot = lax.broadcasted_iota(jnp.int32, (1, total), 1)
    tile = divided(slot, slots)
    carried = jnp.concatenate(
        [
            tile.astype(jnp.float32), (slot - tile * slots).astype(jnp.float32), entry, owner,
            member, low, cols.astype(jnp.float32),
        ],
        axis=0,
    ).astype(jnp.bfloat16)
    at = lax.broadcasted_iota(jnp.int32, (total, total), 0)
    for which in range(3):
        count = counts[which : which + 1]
        wanted = jnp.where(at < count, at, 0)
        chosen = jnp.where(wanted == rank[which : which + 1], 1.0, 0.0).astype(jnp.bfloat16)
        listed = lax.dot_general(carried, chosen, NT, preferred_element_type=jnp.float32)
        listed = listed.astype(jnp.int32)
        (far_slot_ref, slot_ref, own_slot_ref)[which][...] = (listed[0:1] * slots + listed[1:2])[0]
        if which == 1:
            entry_ref[...] = (listed[2:3] + (listed[5:6] - 1) * (2 * per_peer))[0]
            tile_ref[...] = listed[0]
        row = (listed[4:5], listed[3:4] * rows + listed[4:5], listed[6:7])[which]
        row = jnp.where(slot < count, row, -1)
        if which == 2:
            row_ref[...] = row
        else:
            target_ref[which : which + 1, :] = row

    index_ref[...] = jnp.full(index_ref.shape, -1.0, jnp.float32)
    groups = fetch_ref.shape[1] // per_peer
    for p in range(groups):
        part = within[:, p * per_peer : (p + 1) * per_peer].astype(jnp.float32)
        group = jnp.max(
            jnp.where(ghost_lane == p * per_peer, divided(fetched, group_size), 0)
        )
        index_ref[group, :, 0:per_peer] = part
        index_ref[group, :, per_peer : 2 * per_peer] = part


def terms_of(parts, spread, lane_block):
    mode_count = parts[0][0].shape[0]
    halves = [[] for _ in range(mode_count // BATCH)]
    for b in range(len(parts) // BATCH):
        part = parts[b * BATCH : (b + 1) * BATCH]
        block = lax.dot_general(
            jnp.concatenate([s for s, _ in part], axis=0),
            jnp.concatenate([q for _, q in part[::-1]], axis=0),
            NT,
            preferred_element_type=jnp.float32,
        )
        for j in range(BATCH):
            for half in range(mode_count // BATCH):
                row = j * mode_count + half * BATCH
                value = pltpu.roll(block[row : row + BATCH], 0, 1, stride=mode_count, stride_axis=0)
                value = jnp.where(lane_block == BATCH - 1 - j, value, 0.0)
                halves[half].append(value)
    halves = [jnp.concatenate(h, axis=0).astype(jnp.bfloat16) for h in halves]
    flat = jnp.dot(spread, jnp.concatenate(halves, axis=1), preferred_element_type=jnp.float32)
    rows = []
    for b in range(len(parts) // BATCH):
        row = flat[b * BATCH : (b + 1) * BATCH]
        rows.append(
            jnp.concatenate(
                [
                    pltpu.roll(row[:, h * LANES : (h + 1) * LANES], mode_count, 1, stride=mode_count, stride_axis=0)
                    for h in range(len(halves))
                ],
                axis=1,
            )
        )
    return jnp.concatenate(rows, axis=0)


def term_constants(count, mode_count):
    spread = lax.broadcasted_iota(jnp.int32, (count, count * BATCH), 1) // BATCH
    spread = spread == lax.broadcasted_iota(jnp.int32, (count, count * BATCH), 0)
    lane_block = (
        lax.broadcasted_iota(jnp.int32, (BATCH, LANES), 1) // mode_count
        - lax.broadcasted_iota(jnp.int32, (BATCH, LANES), 0)
    ) & (BATCH - 1)
    return jnp.where(spread, 1.0, 0.0).astype(jnp.bfloat16), lane_block


def product_pair(picked, tiles):
    zero = jnp.zeros_like(picked[0])
    left = jnp.concatenate(
        [
            jnp.concatenate([picked[0], zero], axis=1),
            jnp.concatenate([zero, picked[1]], axis=1),
        ],
        axis=0,
    )
    right = jnp.concatenate(tiles, axis=1)
    both = lax.dot_general(left, right, NT, preferred_element_type=jnp.float32)
    rows = picked[0].shape[0]
    return both[:rows], both[rows:]


def summed(one_hot_rows, place, terms, tile_rows):
    one_hot = lax.broadcasted_iota(jnp.int32, (one_hot_rows, place.shape[1]), 0) == place
    one_hot = jnp.where(one_hot, 1.0, 0.0).astype(jnp.bfloat16)
    sums = jnp.dot(one_hot, terms.astype(jnp.bfloat16), preferred_element_type=jnp.float32)
    return sums * (1.0 / tile_rows)


def own_kernel(
    slots, pitch, half, place, far_slot, counts_ref, here, target_ref, index_ref, table_ref, a_hbm,
    prolong_ref, weight_ref, product_ref, first_ref, second_ref, extra_ref, rest_ref, a_ref, terms_ref, arrived,
):
    tile_dev = weight_ref.shape[0]
    mode_count, tile_rows = table_ref.shape[1:]
    pair = 4
    per_step = pair * slots
    steps = tile_dev // pair
    batch = 2 * BATCH
    diagonal = lax.broadcasted_iota(jnp.int32, (tile_rows, tile_rows), 0) == lax.broadcasted_iota(
        jnp.int32, (tile_rows, tile_rows), 1
    )

    def fetch(step):
        part = pl.ds(step * per_step, per_step)
        return pltpu.make_async_copy(a_hbm.at[part], a_ref.at[part], arrived.at[step])

    @pl.loop(0, steps)
    def _(step):
        fetch(step).start()

    total = tile_dev * slots
    terms_ref[...] = jnp.zeros_like(terms_ref)
    rest_ref[...] = jnp.zeros_like(rest_ref)
    groups = index_ref.shape[0]
    height, extra = extra_ref.shape
    rows = height // groups
    far_rows = -(-pitch // 8) * 8
    place_row = lax.broadcasted_iota(jnp.int32, (height, total), 0)
    goal = target_ref[1:2, :]
    first_ref[...] = jnp.where(place_row == goal, 1.0, 0.0).astype(jnp.bfloat16)
    goal = jnp.where(goal >= 0, goal + pitch, -1)
    second_ref[...] = jnp.where(place_row == goal, 1.0, 0.0).astype(jnp.bfloat16)
    row = lax.broadcasted_iota(jnp.int32, (height, extra), 0)
    lane = lax.broadcasted_iota(jnp.int32, (height, extra), 1)
    far_row = (here[0] ^ half) * rows
    chosen = (lane < groups) & (row == lane * rows + 2 * pitch)
    for part in range(2):
        at = lane - groups - part * far_rows
        chosen = chosen | ((at >= 0) & (at < pitch) & (row == far_row + part * pitch + at))
    extra_ref[...] = jnp.where(chosen, 1.0, 0.0).astype(jnp.bfloat16)
    for group in range(groups):
        rest_ref[group : group + 1, :] = index_ref[group][:, 0:LANES] * tile_rows

    @pl.loop(0, steps)
    def _(step):
        fetch(step).wait()
        for i in range(pair):
            tile = step * pair + i
            lead = a_ref[tile * slots].astype(jnp.float32)
            entries = jnp.sum(jnp.where(diagonal, lead, 0.0), axis=0, keepdims=True)
            weight = damping * (1.0 / entries)
            weight_ref[tile] = weight
            for k in range(0, slots, 2):
                slot = tile * slots + k
                picked = [table_ref[place[slot]], table_ref[place[slot + 1]]]
                products = product_pair(picked, [a_ref[slot], a_ref[slot + 1]])
                for d, product in enumerate(products):
                    smooth = -(weight * product)
                    if k + d == 0:
                        smooth = picked[0].astype(jnp.float32) + smooth
                    prolong_ref[slot + d] = smooth.astype(jnp.bfloat16)
                    product_ref[slot + d] = product.astype(jnp.bfloat16)

    spread, lane_block = term_constants(batch, mode_count)

    @pl.loop(0, (counts_ref[0, 0] + batch - 1) // batch)
    def _(step):
        slot = [far_slot[step * batch + i] for i in range(batch)]
        parts = [(prolong_ref[f], product_ref[f]) for f in slot]
        row = pl.multiple_of(step * batch, batch)
        terms_ref[pl.ds(row, batch), :] = terms_of(parts, spread, lane_block)

    sums = summed(far_rows, target_ref[0:1, :], terms_ref[0:total, :], 1)
    rest_ref[groups : groups + far_rows, :] = sums[:, :LANES]
    rest_ref[groups + far_rows : groups + 2 * far_rows, :] = sums[:, LANES:]


def terms_kernel(slots, counts_ref, row_ref, prolong_ref, product_ref, sums_ref, terms_ref):
    total, mode_count, tile_rows = prolong_ref.shape
    batch = 6 * BATCH
    spread, lane_block = term_constants(batch, mode_count)
    terms_ref[...] = jnp.zeros_like(terms_ref)

    @pl.loop(0, (counts_ref[2, 0] + batch - 1) // batch)
    def _(step):
        first = step * batch
        slot = [slots[jnp.minimum(first + i, total - 1)] for i in range(batch)]
        parts = [(prolong_ref[f], product_ref[f]) for f in slot]
        terms_ref[pl.ds(pl.multiple_of(first, BATCH), batch), :] = terms_of(parts, spread, lane_block)

    sums = summed(sums_ref.shape[0], row_ref[...], terms_ref[0:total, :], tile_rows)
    sums_ref[...] = sums.astype(jnp.bfloat16)


def ghost_kernel(
    half, slots, entries, tiles, counts_ref, first_ref, second_ref, extra_ref, rest_ref, a_ref, weight_ref,
    old_ref, *refs,
):
    received = refs[: half - 1]
    prolong_ref, out_ref, table_ref, smooth_ref, product_ref, terms_ref = refs[half - 1 :]
    mode_count, tile_rows = table_ref.shape[1:]
    for s, part_ref in enumerate(received):
        count = part_ref.shape[0]
        table_ref[s * count : (s + 1) * count] = part_ref[...]
    groups, copies, rows, width = out_ref.shape
    total = a_ref.shape[0]
    batch = 2 * BATCH
    spread, lane_block = term_constants(batch, mode_count)
    terms_ref[...] = jnp.zeros_like(terms_ref)
    count = counts_ref[1, 0]
    steps = (count + batch - 1) // batch

    def begin(step):
        first = step * batch
        for i in range(0, batch, 2):
            slot = [slots[first + i + d] for d in range(2)]
            picked = [table_ref[entries[first + i + d]] for d in range(2)]
            products = product_pair(picked, [a_ref[f] for f in slot])
            for d, product in enumerate(products):
                weight = weight_ref[tiles[first + i + d]]
                smooth = (-(weight * product)).astype(jnp.bfloat16)
                prolong_ref[slot[d]] = smooth
                smooth_ref[i + d] = smooth
                product_ref[i + d] = product.astype(jnp.bfloat16)

    def finish(step):
        parts = [(smooth_ref[i], product_ref[i]) for i in range(batch)]
        row = pl.multiple_of(step * batch, batch)
        terms_ref[pl.ds(row, batch), :] = terms_of(parts, spread, lane_block)

    begin(0)

    @pl.loop(1, steps)
    def _(step):
        finish(step - 1)
        begin(step)

    finish(steps - 1)
    terms = terms_ref[0:total, :].astype(jnp.bfloat16)
    result = jnp.dot(first_ref[...], terms[:, :LANES], preferred_element_type=jnp.float32)
    result = result + jnp.dot(second_ref[...], terms[:, LANES:], preferred_element_type=jnp.float32)
    result = result + jnp.dot(
        extra_ref[...], rest_ref[...].astype(jnp.bfloat16), preferred_element_type=jnp.float32
    )
    result = (result * (1.0 / tile_rows)).reshape(groups, rows, width).astype(jnp.bfloat16)
    for copy in range(copies):
        out_ref[:, copy] = result


def target_kernel(pitch, incoming_ref, out_ref):
    senders, rows, width = incoming_ref.shape
    group_size = out_ref.shape[0]
    tile = lax.broadcasted_iota(jnp.int32, (group_size, rows), 0)
    lane = lax.broadcasted_iota(jnp.int32, (group_size, rows), 1)
    totals = [jnp.zeros((group_size, width), jnp.float32) for _ in range(2)]
    for sender in range(senders):
        value = incoming_ref[sender]
        wanted = value[2 * pitch : 2 * pitch + 1, :rows].astype(jnp.float32).astype(jnp.int32)
        match = tile == wanted
        for part in range(2):
            here = match & (lane >= part * pitch) & (lane < (part + 1) * pitch)
            one_hot = jnp.where(here, 1.0, 0.0).astype(jnp.bfloat16)
            totals[part] = totals[part] + jnp.dot(one_hot, value, preferred_element_type=jnp.float32)
    for part, total in enumerate(totals):
        out_ref[:, part * width : (part + 1) * width] = total.astype(jnp.bfloat16)


def shards(a_tiles, modes, col_tiles, fetch_list):
    blk_count = lax.axis_size("blk")
    sub_count = lax.axis_size("sub")
    tile_dev, slot_count, tile_rows = a_tiles.shape[:3]
    mode_count = modes.shape[1]
    width = mode_count * mode_count
    group_size = tile_dev * blk_count
    ghost_count = fetch_list.shape[1]
    peer_count = min(NEIGHBOURS, sub_count - 1)
    per_peer = ghost_count // peer_count
    slot_total = tile_dev * slot_count
    half = sub_count // 2
    blk_half = blk_count // 2
    me = lax.axis_index("sub")
    lane = lax.axis_index("blk")

    far = xor_permute(modes, "sub", half)
    bits = []
    bit = blk_half
    own_part, far_part = [modes], [far]
    while bit:
        own_part = own_part + [xor_permute(part, "blk", bit) for part in own_part]
        far_part = far_part + [xor_permute(part, "blk", bit) for part in far_part]
        bits.append(bit)
        bit //= 2
    blank = jnp.zeros((1, mode_count, tile_rows), modes.dtype)
    table = jnp.concatenate(own_part + far_part + [blank], axis=0)

    theirs = []
    for peer in range(1, half):
        theirs.append(xor_permute(fetch_list, "sub", peer))
    theirs = jnp.concatenate(theirs, axis=0)
    owners = theirs // group_size
    places = table_place(theirs % group_size, lane, tile_dev, bits)
    places = places + jnp.where(owners == (me ^ half), group_size, 0)
    here = jnp.stack([me, lane]).astype(jnp.int32)
    picks = pl.pallas_call(
        functools.partial(pick_kernel, per_peer, half),
        out_shape=[jax.ShapeDtypeStruct((2 * per_peer, mode_count, tile_rows), modes.dtype)] * (half - 1),
        in_specs=[SMEM, SMEM, SMEM, VMEM],
        out_specs=[VMEM] * (half - 1),
        name="pick",
        compiler_params=PARAMS,
    )(here, owners[:, ::per_peer], places, table)
    received = []
    for peer in range(1, half):
        received.append(xor_permute(picks[peer - 1], "sub", peer))

    rows = -(-(2 * per_peer + 1) // 8) * 8
    columns = col_tiles.reshape(1, slot_total)
    place, own_row, far_slot, slot, own_slot, entry, tile, counts, target, index_rows = pl.pallas_call(
        functools.partial(prep_kernel, slot_count, tile_dev, per_peer, rows, half, tuple(bits)),
        out_shape=[
            jax.ShapeDtypeStruct((slot_total,), jnp.int32),
            jax.ShapeDtypeStruct((1, slot_total), jnp.int32),
            *[jax.ShapeDtypeStruct((slot_total,), jnp.int32)] * 5,
            jax.ShapeDtypeStruct((8, LANES), jnp.int32),
            jax.ShapeDtypeStruct((2, slot_total), jnp.int32),
            jax.ShapeDtypeStruct((sub_count, 1, width), jnp.float32),
        ],
        in_specs=[SMEM, VMEM, VMEM],
        out_specs=[VMEM] * 10,
        name="prep",
        compiler_params=PARAMS,
    )(here, columns, fetch_list)

    tiles = a_tiles.reshape(slot_total, tile_rows, tile_rows)
    tiles = pltpu.with_memory_space_constraint(tiles, pltpu.HBM)
    extra = -(-(sub_count + 2 * (-(-per_peer // 8) * 8)) // 32) * 32
    terms_scratch = pltpu.VMEM((slot_total + 2 * BATCH, width), jnp.float32)
    vectors = (slot_total, mode_count, tile_rows)
    prolong, weight, product, first, second, added, rest, tiles = pl.pallas_call(
        functools.partial(own_kernel, slot_count, per_peer, half),
        out_shape=[
            pltpu.VMEM(vectors, jnp.bfloat16),
            jax.ShapeDtypeStruct((tile_dev, 1, tile_rows), jnp.float32),
            pltpu.VMEM(vectors, jnp.bfloat16),
            *[jax.ShapeDtypeStruct((sub_count * rows, slot_total), jnp.bfloat16)] * 2,
            jax.ShapeDtypeStruct((sub_count * rows, extra), jnp.bfloat16),
            jax.ShapeDtypeStruct((extra, LANES), jnp.float32),
            pltpu.VMEM((slot_total, tile_rows, tile_rows), jnp.bfloat16),
        ],
        in_specs=[SMEM] * 4 + [VMEM] * 3 + [pl.BlockSpec(memory_space=pltpu.HBM)],
        out_specs=[VMEM] * 8,
        scratch_shapes=[terms_scratch, pltpu.SemaphoreType.DMA((tile_dev // 4,))],
        name="own",
        compiler_params=PARAMS,
    )(place, far_slot, counts, here, target, index_rows, table, tiles)

    prolong = pltpu.with_memory_space_constraint(prolong, pltpu.VMEM)
    product = pltpu.with_memory_space_constraint(product, pltpu.VMEM)
    tiles = pltpu.with_memory_space_constraint(tiles, pltpu.VMEM)
    prolong, outgoing = pl.pallas_call(
        functools.partial(ghost_kernel, half),
        out_shape=[
            pltpu.VMEM(vectors, jnp.bfloat16),
            jax.ShapeDtypeStruct((sub_count, blk_half, rows, LANES), jnp.bfloat16),
        ],
        in_specs=[SMEM] * 4 + [VMEM] * (7 + half - 1),
        out_specs=[VMEM, VMEM],
        input_output_aliases={10: 0},
        scratch_shapes=[
            pltpu.VMEM((2 * per_peer * (half - 1), mode_count, tile_rows), jnp.bfloat16),
            pltpu.VMEM((2 * BATCH, mode_count, tile_rows), jnp.bfloat16),
            pltpu.VMEM((2 * BATCH, mode_count, tile_rows), jnp.bfloat16),
            terms_scratch,
        ],
        name="ghost",
        compiler_params=GHOST_PARAMS,
    )(
        slot, entry, tile, counts, first, second, added, rest, tiles, weight, prolong, *received,
    )
    finished = pltpu.with_memory_space_constraint(prolong, pltpu.VMEM)

    groups = [
        [s * blk_count + high * 2 + core for s in range(sub_count) for high in range(blk_half)]
        for core in range(2)
    ]
    incoming = lax.all_to_all(
        outgoing.reshape(sub_count * blk_half, rows, LANES),
        ("sub", "blk"), split_axis=0, concat_axis=0, axis_index_groups=groups, tiled=True,
    )

    own_total = pl.pallas_call(
        terms_kernel,
        out_shape=jax.ShapeDtypeStruct((group_size, width), jnp.bfloat16),
        in_specs=[SMEM] * 2 + [VMEM] * 3,
        out_specs=VMEM,
        scratch_shapes=[pltpu.VMEM((slot_total + 6 * BATCH, width), jnp.float32)],
        name="terms",
        compiler_params=PARAMS,
    )(own_slot, counts, own_row, finished, product)
    bit = blk_half
    while bit:
        other = xor_permute(own_total, "blk", bit)
        own_total = own_total.astype(jnp.float32) + other.astype(jnp.float32)
        bit //= 2
        if bit:
            own_total = own_total.astype(jnp.bfloat16)
    arrived = pl.pallas_call(
        functools.partial(target_kernel, per_peer),
        out_shape=jax.ShapeDtypeStruct((group_size, width), jnp.bfloat16),
        in_specs=[VMEM],
        out_specs=VMEM,
        name="target",
        compiler_params=PARAMS,
    )(incoming)
    other = xor_permute(arrived, "blk", 1)
    coarse_diag = own_total + (arrived.astype(jnp.float32) + other.astype(jnp.float32))
    return prolong.reshape(tile_dev, slot_count, mode_count, tile_rows), coarse_diag


def solution(mesh):
    in_specs = (
        P(("sub", "blk"), None, None, None),
        P(("sub", "blk"), None, None),
        P(("sub", "blk"), None),
        P(("sub", "blk"), None),
    )
    out_specs = (P(("sub", "blk"), None, None, None), P("sub", None))

    return jax.shard_map(shards, mesh=mesh, in_specs=in_specs, out_specs=out_specs, check_vma=False)
```

```python
import functools

import jax
import jax.numpy as jnp
from jax import lax
from jax.experimental import pallas as pl
from jax.experimental.pallas import tpu as pltpu
from jax.sharding import PartitionSpec as P


NEIGHBOURS = 26
LANES = 128
BATCH = 8

damping = 2.0 / 3.0


VMEM = pl.BlockSpec(memory_space=pltpu.VMEM)
SMEM = pl.BlockSpec(memory_space=pltpu.SMEM)
PARAMS = pltpu.CompilerParams(vmem_limit_bytes=8 << 20)
GHOST_PARAMS = pltpu.CompilerParams(vmem_limit_bytes=8 << 20)
NT = (((1,), (1,)), ((), ()))


def xor_permute(x, axis, bit):
    count = lax.axis_size(axis)
    return lax.ppermute(x, axis, [(i, i ^ bit) for i in range(count)])


def divided(value, by):
    return jnp.floor((value.astype(jnp.float32) + 0.5) * (1.0 / by)).astype(jnp.int32)


def table_place(within, lane, tile_dev, bits):
    relative = divided(within, tile_dev)
    rest = within - relative * tile_dev
    relative = relative ^ lane
    order = jnp.zeros_like(relative)
    for i, bit in enumerate(bits):
        order = order + jnp.where((relative & bit) != 0, 1 << i, 0)
    return order * tile_dev + rest


def pick_kernel(count, half, here, owner_ref, place_ref, table_ref, *out_refs):
    for peer, out_ref in enumerate(out_refs):
        near = away = 0
        for p in range(owner_ref.shape[1]):
            owner = owner_ref[peer, p]
            near = jnp.where(owner == here[0], p * count, near)
            away = jnp.where(owner == here[0] ^ half, p * count, away)

        @pl.loop(0, count, unroll=2)
        def _(i):
            out_ref[i] = table_ref[place_ref[peer, near + i]]
            out_ref[count + i] = table_ref[place_ref[peer, away + i]]


def prep_kernel(
    slots, tile_dev, per_peer, rows, half, bits, here,
    cols_ref, fetch_ref, place_ref, row_ref, far_slot_ref, slot_ref, own_slot_ref, entry_ref, tile_ref, counts_ref,
    target_ref, index_ref,
):
    me, lane = here[0], here[1]
    total, ghosts = cols_ref.shape[1], fetch_ref.shape[1]
    group_size = tile_dev * (2 ** len(bits))
    fetched = fetch_ref[...]
    owner = divided(fetched, group_size)
    within = fetched - owner * group_size
    apart = owner ^ me
    low = apart & (half - 1)
    ghost_lane = lax.broadcasted_iota(jnp.int32, (1, ghosts), 1)
    member = ghost_lane - divided(ghost_lane, per_peer) * per_peer
    entry = jnp.where(
        low == 0,
        table_place(within, lane, tile_dev, bits),
        jnp.where(apart >= half, per_peer, 0) + member,
    )
    known = jnp.concatenate([low, entry, owner, member], axis=0).astype(jnp.float32)
    known = known.astype(jnp.bfloat16)
    cols = cols_ref[...]
    match = lax.broadcasted_iota(jnp.int32, (ghosts, total), 0) == cols - group_size
    match = jnp.where(match, 1.0, 0.0).astype(jnp.bfloat16)
    found = jnp.dot(known, match, preferred_element_type=jnp.float32)
    low, entry, owner, member = (found[i : i + 1] for i in range(4))
    is_ghost = cols >= group_size
    source = jnp.where(is_ghost, low.astype(jnp.int32), -1)
    entry_int = entry.astype(jnp.int32)
    place_ref[...] = jnp.where(
        source < 0,
        table_place(cols, lane, tile_dev, bits),
        jnp.where(source == 0, group_size + entry_int, 2 * group_size),
    )[0]

    kind = lax.broadcasted_iota(jnp.int32, (8, total), 0)
    chosen = jnp.where(source > 0, 1, jnp.where(source == 0, 0, 2))
    by_kind = jnp.where(kind == chosen, 1.0, 0.0)
    before = lax.broadcasted_iota(jnp.int32, (total, total), 0) < lax.broadcasted_iota(
        jnp.int32, (total, total), 1
    )
    before = jnp.where(before, 1.0, 0.0).astype(jnp.bfloat16)
    rank = jnp.dot(by_kind.astype(jnp.bfloat16), before, preferred_element_type=jnp.float32)
    rank = jnp.where(by_kind > 0.5, rank, -1.0).astype(jnp.int32)
    counts = jnp.sum(by_kind, axis=1, keepdims=True).astype(jnp.int32)
    counts_ref[...] = jnp.broadcast_to(counts, counts_ref.shape)

    slot = lax.broadcasted_iota(jnp.int32, (1, total), 1)
    tile = divided(slot, slots)
    carried = jnp.concatenate(
        [
            tile.astype(jnp.float32), (slot - tile * slots).astype(jnp.float32), entry, owner,
            member, low, cols.astype(jnp.float32),
        ],
        axis=0,
    ).astype(jnp.bfloat16)
    at = lax.broadcasted_iota(jnp.int32, (total, total), 0)
    for which in range(3):
        count = counts[which : which + 1]
        wanted = jnp.where(at < count, at, 0)
        chosen = jnp.where(wanted == rank[which : which + 1], 1.0, 0.0).astype(jnp.bfloat16)
        listed = lax.dot_general(carried, chosen, NT, preferred_element_type=jnp.float32)
        listed = listed.astype(jnp.int32)
        (far_slot_ref, slot_ref, own_slot_ref)[which][...] = (listed[0:1] * slots + listed[1:2])[0]
        if which == 1:
            entry_ref[...] = (listed[2:3] + (listed[5:6] - 1) * (2 * per_peer))[0]
            tile_ref[...] = listed[0]
        row = (listed[4:5], listed[3:4] * rows + listed[4:5], listed[6:7])[which]
        row = jnp.where(slot < count, row, -1)
        if which == 2:
            row_ref[...] = row
        else:
            target_ref[which : which + 1, :] = row

    index_ref[...] = jnp.full(index_ref.shape, -1.0, jnp.float32)
    groups = fetch_ref.shape[1] // per_peer
    for p in range(groups):
        part = within[:, p * per_peer : (p + 1) * per_peer].astype(jnp.float32)
        group = jnp.max(
            jnp.where(ghost_lane == p * per_peer, divided(fetched, group_size), 0)
        )
        index_ref[group, :, 0:per_peer] = part
        index_ref[group, :, per_peer : 2 * per_peer] = part


def terms_of(parts, spread, lane_block):
    mode_count = parts[0][0].shape[0]
    halves = [[] for _ in range(mode_count // BATCH)]
    for b in range(len(parts) // BATCH):
        part = parts[b * BATCH : (b + 1) * BATCH]
        block = lax.dot_general(
            jnp.concatenate([s for s, _ in part], axis=0),
            jnp.concatenate([q for _, q in part[::-1]], axis=0),
            NT,
            preferred_element_type=jnp.float32,
        )
        for j in range(BATCH):
            for half in range(mode_count // BATCH):
                row = j * mode_count + half * BATCH
                value = pltpu.roll(block[row : row + BATCH], 0, 1, stride=mode_count, stride_axis=0)
                value = jnp.where(lane_block == BATCH - 1 - j, value, 0.0)
                halves[half].append(value)
    halves = [jnp.concatenate(h, axis=0).astype(jnp.bfloat16) for h in halves]
    flat = jnp.dot(spread, jnp.concatenate(halves, axis=1), preferred_element_type=jnp.float32)
    rows = []
    for b in range(len(parts) // BATCH):
        row = flat[b * BATCH : (b + 1) * BATCH]
        rows.append(
            jnp.concatenate(
                [
                    pltpu.roll(row[:, h * LANES : (h + 1) * LANES], mode_count, 1, stride=mode_count, stride_axis=0)
                    for h in range(len(halves))
                ],
                axis=1,
            )
        )
    return jnp.concatenate(rows, axis=0)


def term_constants(count, mode_count):
    spread = lax.broadcasted_iota(jnp.int32, (count, count * BATCH), 1) // BATCH
    spread = spread == lax.broadcasted_iota(jnp.int32, (count, count * BATCH), 0)
    lane_block = (
        lax.broadcasted_iota(jnp.int32, (BATCH, LANES), 1) // mode_count
        - lax.broadcasted_iota(jnp.int32, (BATCH, LANES), 0)
    ) & (BATCH - 1)
    return jnp.where(spread, 1.0, 0.0).astype(jnp.bfloat16), lane_block


def product_pair(picked, tiles):
    zero = jnp.zeros_like(picked[0])
    left = jnp.concatenate(
        [
            jnp.concatenate([picked[0], zero], axis=1),
            jnp.concatenate([zero, picked[1]], axis=1),
        ],
        axis=0,
    )
    right = jnp.concatenate(tiles, axis=1)
    both = lax.dot_general(left, right, NT, preferred_element_type=jnp.float32)
    rows = picked[0].shape[0]
    return both[:rows], both[rows:]


def summed(one_hot_rows, place, terms, tile_rows):
    one_hot = lax.broadcasted_iota(jnp.int32, (one_hot_rows, place.shape[1]), 0) == place
    one_hot = jnp.where(one_hot, 1.0, 0.0).astype(jnp.bfloat16)
    sums = jnp.dot(one_hot, terms.astype(jnp.bfloat16), preferred_element_type=jnp.float32)
    return sums * (1.0 / tile_rows)


def own_kernel(
    slots, pitch, half, place, far_slot, counts_ref, here, target_ref, index_ref, table_ref, a_hbm,
    prolong_ref, weight_ref, product_ref, first_ref, second_ref, extra_ref, rest_ref, a_ref, terms_ref, arrived,
):
    tile_dev = weight_ref.shape[0]
    mode_count, tile_rows = table_ref.shape[1:]
    pair = 4
    per_step = pair * slots
    steps = tile_dev // pair
    batch = 2 * BATCH
    diagonal = lax.broadcasted_iota(jnp.int32, (tile_rows, tile_rows), 0) == lax.broadcasted_iota(
        jnp.int32, (tile_rows, tile_rows), 1
    )

    def fetch(step):
        part = pl.ds(step * per_step, per_step)
        return pltpu.make_async_copy(a_hbm.at[part], a_ref.at[part], arrived.at[step])

    @pl.loop(0, steps)
    def _(step):
        fetch(step).start()

    total = tile_dev * slots
    terms_ref[...] = jnp.zeros_like(terms_ref)
    rest_ref[...] = jnp.zeros_like(rest_ref)
    groups = index_ref.shape[0]
    height, extra = extra_ref.shape
    rows = height // groups
    far_rows = -(-pitch // 8) * 8
    place_row = lax.broadcasted_iota(jnp.int32, (height, total), 0)
    goal = target_ref[1:2, :]
    first_ref[...] = jnp.where(place_row == goal, 1.0, 0.0).astype(jnp.bfloat16)
    goal = jnp.where(goal >= 0, goal + pitch, -1)
    second_ref[...] = jnp.where(place_row == goal, 1.0, 0.0).astype(jnp.bfloat16)
    row = lax.broadcasted_iota(jnp.int32, (height, extra), 0)
    lane = lax.broadcasted_iota(jnp.int32, (height, extra), 1)
    far_row = (here[0] ^ half) * rows
    chosen = (lane < groups) & (row == lane * rows + 2 * pitch)
    for part in range(2):
        at = lane - groups - part * far_rows
        chosen = chosen | ((at >= 0) & (at < pitch) & (row == far_row + part * pitch + at))
    extra_ref[...] = jnp.where(chosen, 1.0, 0.0).astype(jnp.bfloat16)
    for group in range(groups):
        rest_ref[group : group + 1, :] = index_ref[group][:, 0:LANES] * tile_rows

    @pl.loop(0, steps)
    def _(step):
        fetch(step).wait()
        for i in range(pair):
            tile = step * pair + i
            lead = a_ref[tile * slots].astype(jnp.float32)
            entries = jnp.sum(jnp.where(diagonal, lead, 0.0), axis=0, keepdims=True)
            weight = damping * (1.0 / entries)
            weight_ref[tile] = weight
            for k in range(0, slots, 2):
                slot = tile * slots + k
                picked = [table_ref[place[slot]], table_ref[place[slot + 1]]]
                products = product_pair(picked, [a_ref[slot], a_ref[slot + 1]])
                for d, product in enumerate(products):
                    smooth = -(weight * product)
                    if k + d == 0:
                        smooth = picked[0].astype(jnp.float32) + smooth
                    prolong_ref[slot + d] = smooth.astype(jnp.bfloat16)
                    product_ref[slot + d] = product.astype(jnp.bfloat16)

    spread, lane_block = term_constants(batch, mode_count)

    @pl.loop(0, (counts_ref[0, 0] + batch - 1) // batch)
    def _(step):
        slot = [far_slot[step * batch + i] for i in range(batch)]
        parts = [(prolong_ref[f], product_ref[f]) for f in slot]
        row = pl.multiple_of(step * batch, batch)
        terms_ref[pl.ds(row, batch), :] = terms_of(parts, spread, lane_block)

    sums = summed(far_rows, target_ref[0:1, :], terms_ref[0:total, :], 1)
    rest_ref[groups : groups + far_rows, :] = sums[:, :LANES]
    rest_ref[groups + far_rows : groups + 2 * far_rows, :] = sums[:, LANES:]


def terms_kernel(slots, counts_ref, row_ref, prolong_ref, product_ref, sums_ref, terms_ref):
    total, mode_count, tile_rows = prolong_ref.shape
    batch = 7 * BATCH
    spread, lane_block = term_constants(batch, mode_count)
    terms_ref[...] = jnp.zeros_like(terms_ref)

    @pl.loop(0, (counts_ref[2, 0] + batch - 1) // batch)
    def _(step):
        first = step * batch
        at = [first + i for i in range(batch)]
        if total % batch:
            at = [jnp.minimum(i, total - 1) for i in at]
        slot = [slots[i] for i in at]
        parts = [(prolong_ref[f], product_ref[f]) for f in slot]
        terms_ref[pl.ds(pl.multiple_of(first, BATCH), batch), :] = terms_of(parts, spread, lane_block)

    sums = summed(sums_ref.shape[0], row_ref[...], terms_ref[0:total, :], tile_rows)
    sums_ref[...] = sums.astype(jnp.bfloat16)


def ghost_kernel(
    half, slots, entries, tiles, counts_ref, first_ref, second_ref, extra_ref, rest_ref, a_ref, weight_ref,
    old_ref, *refs,
):
    received = refs[: half - 1]
    prolong_ref, out_ref, table_ref, smooth_ref, product_ref, terms_ref = refs[half - 1 :]
    mode_count, tile_rows = table_ref.shape[1:]
    for s, part_ref in enumerate(received):
        count = part_ref.shape[0]
        table_ref[s * count : (s + 1) * count] = part_ref[...]
    groups, copies, rows, width = out_ref.shape
    total = a_ref.shape[0]
    batch = 2 * BATCH
    spread, lane_block = term_constants(batch, mode_count)
    terms_ref[...] = jnp.zeros_like(terms_ref)
    count = counts_ref[1, 0]
    steps = (count + batch - 1) // batch

    def begin(step):
        first = step * batch
        for i in range(0, batch, 2):
            slot = [slots[first + i + d] for d in range(2)]
            picked = [table_ref[entries[first + i + d]] for d in range(2)]
            products = product_pair(picked, [a_ref[f] for f in slot])
            for d, product in enumerate(products):
                weight = weight_ref[tiles[first + i + d]]
                smooth = (-(weight * product)).astype(jnp.bfloat16)
                prolong_ref[slot[d]] = smooth
                smooth_ref[i + d] = smooth
                product_ref[i + d] = product.astype(jnp.bfloat16)

    def finish(step):
        parts = [(smooth_ref[i], product_ref[i]) for i in range(batch)]
        row = pl.multiple_of(step * batch, batch)
        terms_ref[pl.ds(row, batch), :] = terms_of(parts, spread, lane_block)

    begin(0)

    @pl.loop(1, steps)
    def _(step):
        finish(step - 1)
        begin(step)

    finish(steps - 1)
    terms = terms_ref[0:total, :].astype(jnp.bfloat16)
    result = jnp.dot(first_ref[...], terms[:, :LANES], preferred_element_type=jnp.float32)
    result = result + jnp.dot(second_ref[...], terms[:, LANES:], preferred_element_type=jnp.float32)
    result = result + jnp.dot(
        extra_ref[...], rest_ref[...].astype(jnp.bfloat16), preferred_element_type=jnp.float32
    )
    result = (result * (1.0 / tile_rows)).reshape(groups, rows, width).astype(jnp.bfloat16)
    for copy in range(copies):
        out_ref[:, copy] = result


def target_kernel(pitch, incoming_ref, out_ref):
    senders, rows, width = incoming_ref.shape
    group_size = out_ref.shape[0]
    tile = lax.broadcasted_iota(jnp.int32, (group_size, rows), 0)
    lane = lax.broadcasted_iota(jnp.int32, (group_size, rows), 1)
    totals = [jnp.zeros((group_size, width), jnp.float32) for _ in range(2)]
    for sender in range(senders):
        value = incoming_ref[sender]
        wanted = value[2 * pitch : 2 * pitch + 1, :rows].astype(jnp.float32).astype(jnp.int32)
        match = tile == wanted
        for part in range(2):
            here = match & (lane >= part * pitch) & (lane < (part + 1) * pitch)
            one_hot = jnp.where(here, 1.0, 0.0).astype(jnp.bfloat16)
            totals[part] = totals[part] + jnp.dot(one_hot, value, preferred_element_type=jnp.float32)
    for part, total in enumerate(totals):
        out_ref[:, part * width : (part + 1) * width] = total.astype(jnp.bfloat16)


def shards(a_tiles, modes, col_tiles, fetch_list):
    blk_count = lax.axis_size("blk")
    sub_count = lax.axis_size("sub")
    tile_dev, slot_count, tile_rows = a_tiles.shape[:3]
    mode_count = modes.shape[1]
    width = mode_count * mode_count
    group_size = tile_dev * blk_count
    ghost_count = fetch_list.shape[1]
    peer_count = min(NEIGHBOURS, sub_count - 1)
    per_peer = ghost_count // peer_count
    slot_total = tile_dev * slot_count
    half = sub_count // 2
    blk_half = blk_count // 2
    me = lax.axis_index("sub")
    lane = lax.axis_index("blk")

    far = xor_permute(modes, "sub", half)
    bits = []
    bit = blk_half
    own_part, far_part = [modes], [far]
    while bit:
        own_part = own_part + [xor_permute(part, "blk", bit) for part in own_part]
        far_part = far_part + [xor_permute(part, "blk", bit) for part in far_part]
        bits.append(bit)
        bit //= 2
    blank = jnp.zeros((1, mode_count, tile_rows), modes.dtype)
    table = jnp.concatenate(own_part + far_part + [blank], axis=0)

    theirs = []
    for peer in range(1, half):
        theirs.append(xor_permute(fetch_list, "sub", peer))
    theirs = jnp.concatenate(theirs, axis=0)
    owners = theirs // group_size
    places = table_place(theirs % group_size, lane, tile_dev, bits)
    places = places + jnp.where(owners == (me ^ half), group_size, 0)
    here = jnp.stack([me, lane]).astype(jnp.int32)
    picks = pl.pallas_call(
        functools.partial(pick_kernel, per_peer, half),
        out_shape=[jax.ShapeDtypeStruct((2 * per_peer, mode_count, tile_rows), modes.dtype)] * (half - 1),
        in_specs=[SMEM, SMEM, SMEM, VMEM],
        out_specs=[VMEM] * (half - 1),
        name="pick",
        compiler_params=PARAMS,
    )(here, owners[:, ::per_peer], places, table)
    received = []
    for peer in range(1, half):
        received.append(xor_permute(picks[peer - 1], "sub", peer))

    rows = -(-(2 * per_peer + 1) // 8) * 8
    columns = col_tiles.reshape(1, slot_total)
    place, own_row, far_slot, slot, own_slot, entry, tile, counts, target, index_rows = pl.pallas_call(
        functools.partial(prep_kernel, slot_count, tile_dev, per_peer, rows, half, tuple(bits)),
        out_shape=[
            jax.ShapeDtypeStruct((slot_total,), jnp.int32),
            jax.ShapeDtypeStruct((1, slot_total), jnp.int32),
            *[jax.ShapeDtypeStruct((slot_total,), jnp.int32)] * 5,
            jax.ShapeDtypeStruct((8, LANES), jnp.int32),
            jax.ShapeDtypeStruct((2, slot_total), jnp.int32),
            jax.ShapeDtypeStruct((sub_count, 1, width), jnp.float32),
        ],
        in_specs=[SMEM, VMEM, VMEM],
        out_specs=[VMEM] * 10,
        name="prep",
        compiler_params=PARAMS,
    )(here, columns, fetch_list)

    tiles = a_tiles.reshape(slot_total, tile_rows, tile_rows)
    tiles = pltpu.with_memory_space_constraint(tiles, pltpu.HBM)
    extra = -(-(sub_count + 2 * (-(-per_peer // 8) * 8)) // 32) * 32
    terms_scratch = pltpu.VMEM((slot_total + 2 * BATCH, width), jnp.float32)
    vectors = (slot_total, mode_count, tile_rows)
    prolong, weight, product, first, second, added, rest, tiles = pl.pallas_call(
        functools.partial(own_kernel, slot_count, per_peer, half),
        out_shape=[
            pltpu.VMEM(vectors, jnp.bfloat16),
            jax.ShapeDtypeStruct((tile_dev, 1, tile_rows), jnp.float32),
            pltpu.VMEM(vectors, jnp.bfloat16),
            *[jax.ShapeDtypeStruct((sub_count * rows, slot_total), jnp.bfloat16)] * 2,
            jax.ShapeDtypeStruct((sub_count * rows, extra), jnp.bfloat16),
            jax.ShapeDtypeStruct((extra, LANES), jnp.float32),
            pltpu.VMEM((slot_total, tile_rows, tile_rows), jnp.bfloat16),
        ],
        in_specs=[SMEM] * 4 + [VMEM] * 3 + [pl.BlockSpec(memory_space=pltpu.HBM)],
        out_specs=[VMEM] * 8,
        scratch_shapes=[terms_scratch, pltpu.SemaphoreType.DMA((tile_dev // 4,))],
        name="own",
        compiler_params=PARAMS,
    )(place, far_slot, counts, here, target, index_rows, table, tiles)

    prolong = pltpu.with_memory_space_constraint(prolong, pltpu.VMEM)
    product = pltpu.with_memory_space_constraint(product, pltpu.VMEM)
    tiles = pltpu.with_memory_space_constraint(tiles, pltpu.VMEM)
    prolong, outgoing = pl.pallas_call(
        functools.partial(ghost_kernel, half),
        out_shape=[
            pltpu.VMEM(vectors, jnp.bfloat16),
            jax.ShapeDtypeStruct((sub_count, blk_half, rows, LANES), jnp.bfloat16),
        ],
        in_specs=[SMEM] * 4 + [VMEM] * (7 + half - 1),
        out_specs=[VMEM, VMEM],
        input_output_aliases={10: 0},
        scratch_shapes=[
            pltpu.VMEM((2 * per_peer * (half - 1), mode_count, tile_rows), jnp.bfloat16),
            pltpu.VMEM((2 * BATCH, mode_count, tile_rows), jnp.bfloat16),
            pltpu.VMEM((2 * BATCH, mode_count, tile_rows), jnp.bfloat16),
            terms_scratch,
        ],
        name="ghost",
        compiler_params=GHOST_PARAMS,
    )(
        slot, entry, tile, counts, first, second, added, rest, tiles, weight, prolong, *received,
    )
    finished = pltpu.with_memory_space_constraint(prolong, pltpu.VMEM)

    groups = [
        [s * blk_count + high * 2 + core for s in range(sub_count) for high in range(blk_half)]
        for core in range(2)
    ]
    incoming = lax.all_to_all(
        outgoing.reshape(sub_count * blk_half, rows, LANES),
        ("sub", "blk"), split_axis=0, concat_axis=0, axis_index_groups=groups, tiled=True,
    )

    own_total = pl.pallas_call(
        terms_kernel,
        out_shape=jax.ShapeDtypeStruct((group_size, width), jnp.bfloat16),
        in_specs=[SMEM] * 2 + [VMEM] * 3,
        out_specs=VMEM,
        scratch_shapes=[pltpu.VMEM((slot_total + 7 * BATCH, width), jnp.float32)],
        name="terms",
        compiler_params=PARAMS,
    )(own_slot, counts, own_row, finished, product)
    bit = blk_half
    while bit:
        other = xor_permute(own_total, "blk", bit)
        own_total = own_total.astype(jnp.float32) + other.astype(jnp.float32)
        bit //= 2
        if bit:
            own_total = own_total.astype(jnp.bfloat16)
    arrived = pl.pallas_call(
        functools.partial(target_kernel, per_peer),
        out_shape=jax.ShapeDtypeStruct((group_size, width), jnp.bfloat16),
        in_specs=[VMEM],
        out_specs=VMEM,
        name="target",
        compiler_params=PARAMS,
    )(incoming)
    other = xor_permute(arrived, "blk", 1)
    coarse_diag = own_total + (arrived.astype(jnp.float32) + other.astype(jnp.float32))
    return prolong.reshape(tile_dev, slot_count, mode_count, tile_rows), coarse_diag


def solution(mesh):
    in_specs = (
        P(("sub", "blk"), None, None, None),
        P(("sub", "blk"), None, None),
        P(("sub", "blk"), None),
        P(("sub", "blk"), None),
    )
    out_specs = (P(("sub", "blk"), None, None, None), P("sub", None))

    return jax.shard_map(shards, mesh=mesh, in_specs=in_specs, out_specs=out_specs, check_vma=False)
```
